512 devices in a mesh: seq: 16 (over y, x), table: 32 (over z, core).
Axes of the slice: x: 4, y: 4, z: 16, core: 2. Of those that a mesh axis runs over, the one named last changes fastest.
Arguments:
- events_x: bfloat16 [32, 2048, 512], P('table', 'seq'), may hold values from -6 to 6
- proj: bfloat16 [512, 1536], replicated, may hold values from -0.25 to 0.25
- out_grad: bfloat16 [32, 2048, 512], P('table', 'seq'), may hold values from -6 to 6
- block_mask: int32 [16, 16], replicated, may hold values 0 or 1
- item_ids: int32 [32, 2048], P('table', 'seq'), may hold values from 0 to 16383, as said below
- owner_of: int32 [16384], replicated, may hold values from 0 to 31, as said below
- local_of: int32 [16384], replicated, may hold values from 0 to 511, as said below
- table: bfloat16 [16384, 512], P('table'), may hold values from -3 to 3
- moment: float32 [16384, 512], P('table'), may hold values from -2 to 2
- second: float32 [16384], P('table'), may hold values from 0.05 to 2
Outputs:
- new_table: bfloat16 [16384, 512], P('table')
- new_moment: float32 [16384, 512], P('table')
- new_second: float32 [16384], P('table')
- event_rows: bfloat16 [32, 2048, 512], P('table', 'seq')
The draws below stay inside these ranges and needn't reach their ends.
Inputs may be any that keep to these rules, and one draw needn't show every extreme that they name: `item_ids`: among the 128 events of one device (one history, one seq index), at most 8 have items of one owner (owner_of); in every draw, for each seq index, some owner gets exactly 8 from the device of every history. owner_of[r] * 512 + local_of[r] takes every value of 0 to 16383 once over the items r. `local_of`: see owner_of.
All inputs are finite; a program needn't handle non-finite values.
Results may differ from the reference program's by a relative error of at most 0.0075.
Values may be sent and summed in bfloat16 or wider, within the bound.
No kernel may reach another device: no remote copies, remote signals or barrier semaphores. Data moves between devices by JAX's collectives and lax.ppermute only.
A program may use at most 64 MiB of HBM per device.

```python
import math
import jax
import jax.numpy as jnp
from jax import lax

D = 512
HEADS = 8
HEAD = 64
TOK_DEV = 128
ROWS = 512
SEQ = 2048
BLOCKS = 16
BATCH = 32
ITEMS = 16384
CAP = 8


def slab_layout(key):
    return jax.random.permutation(jax.random.fold_in(key, 11), ITEMS).astype(jnp.int32)


def slab_places(key):
    layout = slab_layout(key)
    return jnp.zeros((ITEMS,), jnp.int32).at[layout].set(jnp.arange(ITEMS, dtype=jnp.int32))


def draw_owner_of(key, part):
    return slab_places(key) // ROWS


def draw_local_of(key, part):
    return slab_places(key) % ROWS


def draw_item_ids(key, part):
    layout = slab_layout(key)
    hottest = jax.random.randint(jax.random.fold_in(key, 5), (BLOCKS,), 0, BATCH).astype(jnp.int32)
    block_hot = jnp.tile(hottest, BATCH)
    block_keys = jax.vmap(lambda number: jax.random.fold_in(jax.random.fold_in(key, 17), number))(jnp.arange(BATCH * BLOCKS))

    def one_block(block_key, hot_owner):
        others = (hot_owner + 1 + jnp.arange((BATCH - 1) * CAP, dtype=jnp.int32) // CAP) % BATCH
        mixed = jax.random.permutation(jax.random.fold_in(block_key, 1), others)[:TOK_DEV - CAP]
        owners = jnp.concatenate([jnp.full((CAP,), hot_owner, jnp.int32), mixed.astype(jnp.int32)])
        owners = jax.random.permutation(jax.random.fold_in(block_key, 2), owners)
        first_pick = jax.random.randint(jax.random.fold_in(block_key, 3), (TOK_DEV,), 0, ROWS)
        second_pick = jax.random.randint(jax.random.fold_in(block_key, 4), (TOK_DEV,), 0, ROWS)
        local_row = first_pick * second_pick // ROWS
        return layout[owners * ROWS + local_row]
    events = jax.vmap(one_block)(block_keys, block_hot)
    return events.reshape(BATCH, SEQ).astype(jnp.int32)


def with_ends(array, rng, low, high):
    extent = array.shape
    index_at = [jax.random.randint(jax.random.fold_in(rng, axis), (), 0, extent[axis]) for axis in range(len(extent))]
    array = array.at[tuple(index_at)].set(low)
    longest = extent.index(max(extent))
    index_at[longest] = (index_at[longest] + 1) % extent[longest]
    return array.at[tuple(index_at)].set(high)


def levels(rng, shape, pieces, smallest, high):
    factor_of, own = 1.0, jax.random.fold_in(rng, 6)
    for dim, parts in pieces:
        steps = jnp.exp(jax.random.uniform(jax.random.fold_in(own, dim), (parts,), jnp.float32, smallest / len(pieces), high / len(pieces)))
        factor_of = factor_of * jnp.repeat(steps, shape[dim] // parts).reshape([-1 if axis == dim else 1 for axis in range(len(shape))])
    return factor_of


def noise(own_key, dims, width, bound, pieces=(), kind=jnp.bfloat16):
    result = jax.random.normal(own_key, dims, jnp.float32) * width
    if len(pieces) > 0:
        result = levels(own_key, dims, pieces, -0.22, 0.18) * result
    return jnp.clip(result, min=-bound, max=bound).astype(kind)


def setup_inputs(seed: int = 0) -> dict:
    key_list = jax.random.split(jax.random.key(seed), 11)
    return {
        "events_x": noise(key_list[0], (BATCH, SEQ, D), 1.0, 6.0, ((0, 32), (1, 16))),
        "proj": noise(key_list[1], (D, 3 * D), D ** -0.5, 0.25),
        "out_grad": noise(key_list[2], (BATCH, SEQ, D), 1.0, 6.0, ((0, 32), (1, 16))),
        "block_mask": with_ends((jax.random.randint(key_list[3], (BLOCKS, BLOCKS), 0, 4) < 3).astype(jnp.int32), jax.random.fold_in(key_list[3], 1), 0, 1),
        "item_ids": draw_item_ids(jax.random.fold_in(key_list[10], 71), 0),
        "owner_of": draw_owner_of(jax.random.fold_in(key_list[10], 71), 0),
        "local_of": draw_local_of(jax.random.fold_in(key_list[10], 71), 0),
        "table": noise(key_list[7], (ITEMS, D), 0.5, 3.0, ((0, 32),)),
        "moment": noise(key_list[8], (ITEMS, D), 0.3, 2.0, ((0, 32),), jnp.float32),
        "second": jnp.clip(jnp.exp(math.log(2.0) - 3.6888794 * jax.random.uniform(key_list[9], (ITEMS,), jnp.float32) ** levels(key_list[9], (ITEMS,), ((0, 32),), -0.2, 0.2)), 0.05, 2.0),
    }


first_decay = 0.9
second_decay = 0.99
step_rate = 0.05
epsilon = 1e-08

def split_heads(matrix):
    return matrix.reshape(SEQ, HEADS, HEAD).transpose(1, 0, 2)

def merge_heads(matrix):
    return matrix.transpose(1, 0, 2).reshape(SEQ, D)

def history_grad(inputs, cotangent, proj, allowed):
    projected = jnp.dot(inputs, proj, preferred_element_type=jnp.float32).astype(jnp.bfloat16)
    query_mat = split_heads(projected[:, :D])
    key_mat = split_heads(projected[:, D:2 * D])
    value_mat = split_heads(projected[:, 2 * D:])
    grad_mat = split_heads(cotangent)
    history_scale = 1.0 / math.sqrt(SEQ)
    temper = 1.0 / math.sqrt(HEAD)

    def per_head(head_parts):
        query_head, key_head, value_head, grad_head = head_parts
        scores = jnp.dot(query_head, key_head.T, preferred_element_type=jnp.float32) * temper
        gates = jax.nn.sigmoid(scores)
        weights = (scores * gates * history_scale * allowed).astype(jnp.bfloat16)
        slopes = gates * (1.0 + scores * (1.0 - gates))
        attn_grad = jnp.dot(grad_head, value_head.T, preferred_element_type=jnp.float32)
        score_grad = (attn_grad * slopes * (history_scale * temper) * allowed).astype(jnp.bfloat16)
        query_grad = jnp.dot(score_grad, key_head, preferred_element_type=jnp.float32)
        key_grad = jnp.dot(score_grad.T, query_head, preferred_element_type=jnp.float32)
        value_grad = jnp.dot(weights.T, grad_head, preferred_element_type=jnp.float32)
        return (query_grad, key_grad, value_grad)
    query_grad, key_grad, value_grad = lax.map(per_head, (query_mat, key_mat, value_mat, grad_mat))
    stacked = jnp.concatenate([merge_heads(query_grad), merge_heads(key_grad), merge_heads(value_grad)], axis=1).astype(jnp.bfloat16)
    return lax.dot_general(stacked, proj, (((1,), (1,)), ((), ())), preferred_element_type=jnp.float32).astype(jnp.bfloat16)

def reference(events_x, proj, out_grad, block_mask, item_ids, owner_of, local_of, table, moment, second):
    block_ids = jnp.arange(BLOCKS)
    visible = (block_mask == 1) | (block_ids[:, None] == block_ids[None, :])
    positions = jnp.arange(SEQ)
    pos_block = positions // TOK_DEV
    allowed = (visible[pos_block][:, pos_block] & (positions[None, :] <= positions[:, None])).astype(jnp.float32)

    def per_history(history_pair):
        return history_grad(history_pair[0], history_pair[1], proj, allowed)
    input_grad = lax.map(per_history, (events_x, out_grad))
    place = (owner_of[item_ids] * ROWS + local_of[item_ids]).astype(jnp.int32).reshape(-1)
    item_grad = jax.ops.segment_sum(input_grad.reshape(-1, D).astype(jnp.float32), place, num_segments=ITEMS)
    new_moment = first_decay * moment + (1.0 - first_decay) * item_grad
    new_second = second_decay * second + (1.0 - second_decay) * lax.optimization_barrier(jnp.mean(item_grad * item_grad, axis=1))
    new_table = (table.astype(jnp.float32) - step_rate * new_moment / (jnp.sqrt(new_second) + epsilon)[:, None]).astype(jnp.bfloat16)
    event_rows = new_table[place].reshape(BATCH, SEQ, D)
    return (new_table, new_moment, new_second, event_rows)
```

```python
import math

import jax
import jax.numpy as jnp
from jax import lax
from jax.experimental import pallas as pl
from jax.experimental.pallas import tpu as pltpu
from jax.sharding import PartitionSpec as P

HEADS = 8
LANES = 128
DIGIT = 16

first_decay = 0.9
second_decay = 0.99
step_rate = 0.05
epsilon = 1e-08

f32 = jnp.float32
bf16 = jnp.bfloat16


def swap_halves(block):
    half = block.shape[1] // 2
    return pltpu.roll(block, half, 1)


def low_lanes(shape):
    return lax.broadcasted_iota(jnp.int32, shape, 1) < shape[1] // 2


def pair_low(first, second):
    return jnp.where(low_lanes(first.shape), first, swap_halves(second))


def pair_high(first, second):
    return jnp.where(low_lanes(first.shape), swap_halves(first), second)


def project_kernel(x_ref, proj_ref, grad_ref, send_ref):
    features = x_ref.shape[1]
    rows = x_ref.shape[0]
    half = rows // 2
    x = x_ref[...]
    for pair in range(HEADS // 2):
        at = pair * LANES
        parts = [
            jnp.dot(
                x, proj_ref[:, third * features + at : third * features + at + LANES],
                preferred_element_type=f32,
            )
            for third in range(3)
        ]
        cot = grad_ref[:, at : at + LANES].astype(f32)
        queries, keys, values = parts
        for odd, join in ((0, pair_low), (1, pair_high)):
            query_grad = join(queries, cot).astype(bf16)
            key_value = join(keys, values).astype(bf16)
            for part in range(2):
                slot = 2 * (2 * pair + odd) + part
                send_ref[slot, 0:rows, :] = query_grad
                send_ref[slot, rows : rows + half, :] = key_value[part * half : part * half + half]


def attention_kernel(part_ref, seen_ref, got_ref, out_ref, key_s, value_s, total_s):
    blocks = got_ref.shape[0]
    rows = out_ref.shape[1]
    half = rows // 2
    tile = 2 * rows
    history_scale = 1.0 / math.sqrt(rows * blocks)
    part = part_ref[0]
    both = got_ref[:, rows : rows + half, :].reshape(blocks * half, LANES)
    low = low_lanes(both.shape)
    zero = jnp.zeros_like(both)
    key_s[...] = jnp.where(low, both * jnp.bfloat16(0.0625), zero)
    value_s[...] = jnp.where(low, zero, both)
    key_row = lax.broadcasted_iota(jnp.int32, (rows, tile), 0)
    query_col = lax.broadcasted_iota(jnp.int32, (rows, tile), 1)
    key_pos = (key_row // half) * rows + part * half + key_row % half
    causal = (key_pos <= query_col).astype(f32)
    for step in range(blocks // 2):
        query_grad = got_ref[2 * step : 2 * step + 2, 0:rows, :].reshape(tile, LANES)
        query_total = jnp.zeros((tile, LANES), f32)
        for chunk in range(step + 1):
            keys = key_s[chunk * rows : chunk * rows + rows, :]
            values = value_s[chunk * rows : chunk * rows + rows, :]
            half_scores = lax.dot_general(
                keys, query_grad, (((1,), (1,)), ((), ())), preferred_element_type=f32
            )
            weight_grad = lax.dot_general(
                values, query_grad, (((1,), (1,)), ((), ())), preferred_element_type=f32
            )
            seen = jnp.concatenate(
                [
                    jnp.broadcast_to(
                        seen_ref[2 * chunk + b : 2 * chunk + b + 1, step * tile : step * tile + tile],
                        (half, tile),
                    )
                    for b in range(2)
                ],
                axis=0,
            )
            if chunk == step:
                seen = seen * causal
            gate2 = (1.0 + jnp.tanh(half_scores)) * seen
            weights = half_scores * gate2
            score_grad = (weight_grad * (gate2 + weights * (2.0 - gate2))).astype(bf16)
            weights = weights.astype(bf16)
            key_part = jnp.dot(score_grad, query_grad, preferred_element_type=f32)
            value_part = jnp.dot(weights, query_grad, preferred_element_type=f32)
            joined = jnp.where(low_lanes(key_part.shape), key_part, value_part)
            if chunk == step:
                total_s[chunk * rows : chunk * rows + rows, :] = joined
            else:
                total_s[chunk * rows : chunk * rows + rows, :] += joined
            query_total += lax.dot_general(
                score_grad, keys, (((0,), (0,)), ((), ())), preferred_element_type=f32
            )
        query_total = query_total * history_scale
        for b in range(2):
            top = query_total[b * rows : b * rows + half]
            bottom = query_total[b * rows + half : b * rows + rows]
            out_ref[2 * step + b, half:rows, :] = (top + swap_halves(bottom)).astype(bf16)
    scale = jnp.where(low_lanes((1, LANES)), history_scale * 0.0625, history_scale)
    out_ref[:, 0:half, :] = (total_s[...] * scale).astype(bf16).reshape(blocks, half, LANES)


def input_grad_kernel(got_ref, proj_ref, target_ref, digits_ref, send_ref):
    rows = got_ref.shape[1]
    half = rows // 2
    queries, keys, values = [], [], []
    for pair in range(HEADS // 2):
        query, joint = [], []
        for odd in range(2):
            slot = 2 * (2 * pair + odd)
            query.append(
                got_ref[slot, half:rows, :].astype(f32) + got_ref[slot + 1, half:rows, :].astype(f32)
            )
            joint.append(
                jnp.concatenate(
                    [got_ref[slot, 0:half, :], got_ref[slot + 1, 0:half, :]], axis=0
                ).astype(f32)
            )
        queries.append(jnp.concatenate([pair_low(*query), pair_high(*query)], axis=0))
        keys.append(pair_low(*joint))
        values.append(pair_high(*joint))
    stacked = jnp.concatenate(queries + keys + values, axis=1).astype(bf16)
    input_grad = lax.dot_general(
        stacked, proj_ref[...], (((1,), (1,)), ((), ())), preferred_element_type=f32
    ).astype(bf16)
    slots = send_ref.shape[0]
    features = input_grad.shape[1]
    onehot = (
        lax.broadcasted_iota(jnp.int32, (slots, rows), 0) == target_ref[...]
    ).astype(f32).astype(bf16)
    send_ref[:, 0:features] = jnp.dot(onehot, input_grad, preferred_element_type=f32).astype(bf16)
    send_ref[:, features:] = jnp.dot(onehot, digits_ref[...], preferred_element_type=f32).astype(bf16)


def slot_rows(digits, slab_rows):
    digits = digits.astype(f32)
    row = digits[:, 0:1] * DIGIT + digits[:, 1:2] - DIGIT
    lane = lax.broadcasted_iota(jnp.int32, (digits.shape[0], slab_rows), 1).astype(f32)
    return (row == lane).astype(f32).astype(bf16)


def slab_kernel(got_ref, slab_ref):
    slab_rows, features = slab_ref.shape
    select = slot_rows(got_ref[:, features:], slab_rows)
    slab_ref[...] = lax.dot_general(
        select, got_ref[:, 0:features], (((0,), (0,)), ((), ())), preferred_element_type=f32
    ).astype(bf16)


def sum_kernel(got_ref, out_ref):
    count = got_ref.shape[0]
    total = got_ref[0].astype(f32)
    for source in range(1, count):
        total += got_ref[source].astype(f32)
    total = total.astype(bf16)
    for target in range(count):
        out_ref[target] = total


def adam_kernel(
    grad_ref, moment_ref, second_ref, table_ref, digits_ref,
    new_table_ref, new_moment_ref, new_second_ref, reply_ref,
):
    item_grad = grad_ref[...].astype(f32)
    new_moment = first_decay * moment_ref[...] + (1.0 - first_decay) * item_grad
    new_moment_ref[...] = new_moment
    mean = jnp.mean(item_grad * item_grad, axis=1, keepdims=True)
    new_second = second_decay * second_ref[...] + (1.0 - second_decay) * mean
    new_second_ref[...] = new_second
    new_table = (
        table_ref[...].astype(f32) - step_rate * new_moment / (jnp.sqrt(new_second) + epsilon)
    ).astype(bf16)
    new_table_ref[...] = new_table
    select = slot_rows(digits_ref[...], new_table.shape[0])
    reply_ref[...] = jnp.dot(select, new_table, preferred_element_type=f32).astype(bf16)


def event_kernel(target_ref, got_ref, out_ref):
    slots = got_ref.shape[0]
    rows = out_ref.shape[0]
    onehot = (
        lax.broadcasted_iota(jnp.int32, (slots, rows), 0) == target_ref[...]
    ).astype(f32).astype(bf16)
    out_ref[...] = lax.dot_general(
        onehot, got_ref[...], (((0,), (0,)), ((), ())), preferred_element_type=f32
    ).astype(bf16)


def shape(dims, kind):
    return jax.ShapeDtypeStruct(dims, kind)


def exchange(array, axis):
    return lax.all_to_all(array, axis, split_axis=0, concat_axis=0, tiled=True)


def body(events_x, proj, out_grad, block_mask, item_ids, owner_of, local_of, table, moment, second):
    tokens = events_x.shape[1]
    features = events_x.shape[2]
    seq_count = lax.axis_size("seq")
    owner_count = lax.axis_size("table")
    position = lax.axis_index("seq")
    slab_rows = table.shape[0]
    capacity = 2 * tokens // owner_count
    slots = owner_count * capacity
    half = tokens // 2

    send = pl.pallas_call(
        project_kernel,
        out_shape=shape((seq_count, tokens + half, LANES), bf16),
        name="project",
    )(events_x[0], proj, out_grad[0])
    got = exchange(send, "seq")

    block_ids = jnp.arange(seq_count)
    query_blk = jnp.arange(seq_count * tokens) // tokens
    visible = (block_mask == 1) | (block_ids[:, None] == block_ids[None, :])
    seen = jnp.repeat(visible.T.astype(f32), tokens, axis=1)
    part = (position % 2).astype(jnp.int32).reshape(1)
    back = pl.pallas_call(
        attention_kernel,
        out_shape=shape((seq_count, tokens, LANES), bf16),
        in_specs=[
            pl.BlockSpec(memory_space=pltpu.SMEM),
            pl.BlockSpec(memory_space=pltpu.VMEM),
            pl.BlockSpec(memory_space=pltpu.VMEM),
        ],
        scratch_shapes=[
            pltpu.VMEM((seq_count * half, LANES), bf16),
            pltpu.VMEM((seq_count * half, LANES), bf16),
            pltpu.VMEM((seq_count * half, LANES), f32),
        ],
        name="attention",
    )(part, seen, got)
    got_back = exchange(back, "seq")

    place_of = owner_of * slab_rows + local_of
    place = place_of[item_ids[0]]
    owners = place // slab_rows
    slab_index = place % slab_rows
    event = jnp.arange(tokens)
    earlier = (owners[:, None] == owners[None, :]) & (event[:, None] < event[None, :])
    rank = jnp.sum(earlier.astype(jnp.int32), axis=0)
    target = (owners * capacity + rank)[None, :]
    lane = jnp.arange(LANES)[None, :]
    digits = jnp.where(
        lane == 0,
        (slab_index // DIGIT + 1)[:, None],
        jnp.where(lane == 1, (slab_index % DIGIT)[:, None], 0),
    ).astype(bf16)
    send_rows = pl.pallas_call(
        input_grad_kernel,
        out_shape=shape((slots, features + LANES), bf16),
        name="input_grad",
    )(got_back, proj, target, digits)
    got_rows = exchange(
        send_rows.reshape(owner_count, capacity, features + LANES), "table"
    ).reshape(slots, features + LANES)

    slab = pl.pallas_call(slab_kernel, out_shape=shape((slab_rows, features), bf16), name="slab")(
        got_rows
    )
    share = slab_rows // seq_count
    parts = exchange(slab.reshape(seq_count, share, features), "seq")
    copies = pl.pallas_call(
        sum_kernel, out_shape=shape((seq_count, share, features), bf16), name="row_sum"
    )(parts)
    item_grad = exchange(copies, "seq").reshape(slab_rows, features)

    new_table, new_moment, new_second, reply = pl.pallas_call(
        adam_kernel,
        out_shape=(
            shape((slab_rows, features), bf16),
            shape((slab_rows, features), f32),
            shape((slab_rows, 1), f32),
            shape((slots, features), bf16),
        ),
        name="adam",
    )(item_grad, moment, second[:, None], table, got_rows[:, features:])
    returned = exchange(reply.reshape(owner_count, capacity, features), "table")
    event_rows = pl.pallas_call(
        event_kernel, out_shape=shape((tokens, features), bf16), name="event_rows"
    )(target, returned.reshape(slots, features))
    return (new_table, new_moment, new_second[:, 0], event_rows[None])


def solution(mesh):
    return jax.shard_map(
        body,
        mesh=mesh,
        in_specs=(
            P("table", "seq", None),
            P(),
            P("table", "seq", None),
            P(),
            P("table", "seq"),
            P(),
            P(),
            P("table", None),
            P("table", None),
            P("table"),
        ),
        out_specs=(P("table", None), P("table", None), P("table"), P("table", "seq", None)),
        check_vma=False,
    )
```

```python
import math

import jax
import jax.numpy as jnp
from jax import lax
from jax.experimental import pallas as pl
from jax.experimental.pallas import tpu as pltpu
from jax.sharding import PartitionSpec as P

HEADS = 8
LANES = 128
DIGIT = 16

first_decay = 0.9
second_decay = 0.99
step_rate = 0.05
epsilon = 1e-08

f32 = jnp.float32
bf16 = jnp.bfloat16


def swap_halves(block):
    half = block.shape[1] // 2
    return pltpu.roll(block, half, 1)


def low_lanes(shape):
    return lax.broadcasted_iota(jnp.int32, shape, 1) < shape[1] // 2


def pair_low(first, second):
    return jnp.where(low_lanes(first.shape), first, swap_halves(second))


def pair_high(first, second):
    return jnp.where(low_lanes(first.shape), swap_halves(first), second)


def project_kernel(x_ref, proj_ref, grad_ref, send_ref):
    features = x_ref.shape[1]
    rows = x_ref.shape[0]
    half = rows // 2
    x = x_ref[...]
    for pair in range(HEADS // 2):
        at = pair * LANES
        parts = [
            jnp.dot(
                x, proj_ref[:, third * features + at : third * features + at + LANES],
                preferred_element_type=f32,
            )
            for third in range(3)
        ]
        cot = grad_ref[:, at : at + LANES].astype(f32)
        queries, keys, values = parts
        for odd, join in ((0, pair_low), (1, pair_high)):
            query_grad = join(queries, cot).astype(bf16)
            key_value = join(keys, values).astype(bf16)
            for part in range(2):
                slot = 2 * (2 * pair + odd) + part
                send_ref[slot, 0:rows, :] = query_grad
                send_ref[slot, rows : rows + half, :] = key_value[part * half : part * half + half]


def attention_kernel(part_ref, seen_ref, got_ref, out_ref, key_s, value_s, total_s):
    blocks = got_ref.shape[0]
    rows = out_ref.shape[1]
    half = rows // 2
    tile = 2 * rows
    history_scale = 1.0 / math.sqrt(rows * blocks)
    part = part_ref[0]
    both = got_ref[:, rows : rows + half, :].reshape(blocks * half, LANES)
    low = low_lanes(both.shape)
    zero = jnp.zeros_like(both)
    key_s[...] = jnp.where(low, both * jnp.bfloat16(0.0625), zero)
    value_s[...] = jnp.where(low, zero, both)
    key_row = lax.broadcasted_iota(jnp.int32, (rows, tile), 0)
    query_col = lax.broadcasted_iota(jnp.int32, (rows, tile), 1)
    key_pos = (key_row // half) * rows + part * half + key_row % half
    causal = (key_pos <= query_col).astype(f32)
    for step in range(blocks // 2):
        query_grad = got_ref[2 * step : 2 * step + 2, 0:rows, :].reshape(tile, LANES)
        query_total = jnp.zeros((tile, LANES), f32)
        for chunk in range(step + 1):
            keys = key_s[chunk * rows : chunk * rows + rows, :]
            values = value_s[chunk * rows : chunk * rows + rows, :]
            half_scores = lax.dot_general(
                keys, query_grad, (((1,), (1,)), ((), ())), preferred_element_type=f32
            )
            weight_grad = lax.dot_general(
                values, query_grad, (((1,), (1,)), ((), ())), preferred_element_type=f32
            )
            seen = jnp.concatenate(
                [
                    jnp.broadcast_to(
                        seen_ref[2 * chunk + b : 2 * chunk + b + 1, step * tile : step * tile + tile],
                        (half, tile),
                    )
                    for b in range(2)
                ],
                axis=0,
            )
            if chunk == step:
                seen = seen * causal
            gate2 = (1.0 + jnp.tanh(half_scores)) * seen
            weights = half_scores * gate2
            score_grad = (weight_grad * (gate2 + weights * (2.0 - gate2))).astype(bf16)
            weights = weights.astype(bf16)
            key_part = jnp.dot(score_grad, query_grad, preferred_element_type=f32)
            value_part = jnp.dot(weights, query_grad, preferred_element_type=f32)
            joined = jnp.where(low_lanes(key_part.shape), key_part, value_part)
            if chunk == step:
                total_s[chunk * rows : chunk * rows + rows, :] = joined
            else:
                total_s[chunk * rows : chunk * rows + rows, :] += joined
            query_total += lax.dot_general(
                score_grad, keys, (((0,), (0,)), ((), ())), preferred_element_type=f32
            )
        query_total = query_total * history_scale
        for b in range(2):
            top = query_total[b * rows : b * rows + half]
            bottom = query_total[b * rows + half : b * rows + rows]
            out_ref[2 * step + b, half:rows, :] = (top + swap_halves(bottom)).astype(bf16)
    scale = jnp.where(low_lanes((1, LANES)), history_scale * 0.0625, history_scale)
    out_ref[:, 0:half, :] = (total_s[...] * scale).astype(bf16).reshape(blocks, half, LANES)


def input_grad_kernel(got_ref, proj_ref, target_ref, digits_ref, send_ref):
    rows = got_ref.shape[1]
    half = rows // 2
    queries, keys, values = [], [], []
    for pair in range(HEADS // 2):
        query, joint = [], []
        for odd in range(2):
            slot = 2 * (2 * pair + odd)
            query.append(
                got_ref[slot, half:rows, :].astype(f32) + got_ref[slot + 1, half:rows, :].astype(f32)
            )
            joint.append(
                jnp.concatenate(
                    [got_ref[slot, 0:half, :], got_ref[slot + 1, 0:half, :]], axis=0
                ).astype(f32)
            )
        queries.append(jnp.concatenate([pair_low(*query), pair_high(*query)], axis=0))
        keys.append(pair_low(*joint))
        values.append(pair_high(*joint))
    stacked = jnp.concatenate(queries + keys + values, axis=1).astype(bf16)
    input_grad = lax.dot_general(
        stacked, proj_ref[...], (((1,), (1,)), ((), ())), preferred_element_type=f32
    ).astype(bf16)
    slots = send_ref.shape[0]
    features = input_grad.shape[1]
    onehot = (
        lax.broadcasted_iota(jnp.int32, (slots, rows), 0) == target_ref[...]
    ).astype(f32).astype(bf16)
    send_ref[:, 0:features] = jnp.dot(onehot, input_grad, preferred_element_type=f32).astype(bf16)
    send_ref[:, features:] = jnp.dot(onehot, digits_ref[...], preferred_element_type=f32).astype(bf16)


def slot_rows(digits, slab_rows):
    digits = digits.astype(f32)
    row = digits[:, 0:1] * DIGIT + digits[:, 1:2] - DIGIT
    lane = lax.broadcasted_iota(jnp.int32, (digits.shape[0], slab_rows), 1).astype(f32)
    return (row == lane).astype(f32).astype(bf16)


def slab_kernel(got_ref, slab_ref):
    slab_rows, features = slab_ref.shape
    select = slot_rows(got_ref[:, features:], slab_rows)
    slab_ref[...] = lax.dot_general(
        select, got_ref[:, 0:features], (((0,), (0,)), ((), ())), preferred_element_type=f32
    ).astype(bf16)


def sum_kernel(got_ref, out_ref):
    count = got_ref.shape[0]
    total = got_ref[0].astype(f32)
    for source in range(1, count):
        total += got_ref[source].astype(f32)
    total = total.astype(bf16)
    for target in range(count):
        out_ref[target] = total


def adam_kernel(
    grad_ref, moment_ref, second_ref, table_ref, digits_ref,
    new_table_ref, new_moment_ref, new_second_ref, reply_ref,
):
    item_grad = grad_ref[...].astype(f32)
    new_moment = first_decay * moment_ref[...] + (1.0 - first_decay) * item_grad
    new_moment_ref[...] = new_moment
    mean = jnp.mean(item_grad * item_grad, axis=1, keepdims=True)
    new_second = second_decay * second_ref[...] + (1.0 - second_decay) * mean
    new_second_ref[...] = new_second
    new_table = (
        table_ref[...].astype(f32) - step_rate * new_moment / (jnp.sqrt(new_second) + epsilon)
    ).astype(bf16)
    new_table_ref[...] = new_table
    select = slot_rows(digits_ref[...], new_table.shape[0])
    reply_ref[...] = jnp.dot(select, new_table, preferred_element_type=f32).astype(bf16)


def event_kernel(target_ref, got_ref, out_ref):
    slots = got_ref.shape[0]
    rows = out_ref.shape[0]
    onehot = (
        lax.broadcasted_iota(jnp.int32, (slots, rows), 0) == target_ref[...]
    ).astype(f32).astype(bf16)
    out_ref[...] = lax.dot_general(
        onehot, got_ref[...], (((0,), (0,)), ((), ())), preferred_element_type=f32
    ).astype(bf16)


def limit(mib):
    return pltpu.CompilerParams(vmem_limit_bytes=mib * 1024 * 1024)


def whole(dims):
    return pl.BlockSpec(dims, lambda i: (0, 0))


def shape(dims, kind):
    return jax.ShapeDtypeStruct(dims, kind)


def exchange(array, axis):
    return lax.all_to_all(array, axis, split_axis=0, concat_axis=0, tiled=True)


def body(events_x, proj, out_grad, block_mask, item_ids, owner_of, local_of, table, moment, second):
    tokens = events_x.shape[1]
    features = events_x.shape[2]
    seq_count = lax.axis_size("seq")
    owner_count = lax.axis_size("table")
    position = lax.axis_index("seq")
    slab_rows = table.shape[0]
    capacity = 2 * tokens // owner_count
    slots = owner_count * capacity
    half = tokens // 2

    send = pl.pallas_call(
        project_kernel,
        out_shape=shape((seq_count, tokens + half, LANES), bf16),
        compiler_params=limit(8), name="project",
    )(events_x[0], proj, out_grad[0])
    got = exchange(send, "seq")

    block_ids = jnp.arange(seq_count)
    query_blk = jnp.arange(seq_count * tokens) // tokens
    visible = (block_mask == 1) | (block_ids[:, None] == block_ids[None, :])
    seen = jnp.repeat(visible.T.astype(f32), tokens, axis=1)
    part = (position % 2).astype(jnp.int32).reshape(1)
    back = pl.pallas_call(
        attention_kernel,
        out_shape=shape((seq_count, tokens, LANES), bf16),
        in_specs=[
            pl.BlockSpec(memory_space=pltpu.SMEM),
            pl.BlockSpec(memory_space=pltpu.VMEM),
            pl.BlockSpec(memory_space=pltpu.VMEM),
        ],
        scratch_shapes=[
            pltpu.VMEM((seq_count * half, LANES), bf16),
            pltpu.VMEM((seq_count * half, LANES), bf16),
            pltpu.VMEM((seq_count * half, LANES), f32),
        ],
        compiler_params=limit(16), name="attention",
    )(part, seen, got)
    got_back = exchange(back, "seq")

    place_of = owner_of * slab_rows + local_of
    place = place_of[item_ids[0]]
    owners = place // slab_rows
    slab_index = place % slab_rows
    event = jnp.arange(tokens)
    earlier = (owners[:, None] == owners[None, :]) & (event[:, None] < event[None, :])
    rank = jnp.sum(earlier.astype(jnp.int32), axis=0)
    target = (owners * capacity + rank)[None, :]
    lane = jnp.arange(LANES)[None, :]
    digits = jnp.where(
        lane == 0,
        (slab_index // DIGIT + 1)[:, None],
        jnp.where(lane == 1, (slab_index % DIGIT)[:, None], 0),
    ).astype(bf16)
    send_rows = pl.pallas_call(
        input_grad_kernel,
        out_shape=shape((slots, features + LANES), bf16),
        compiler_params=limit(12), name="input_grad",
    )(got_back, proj, target, digits)
    got_rows = exchange(
        send_rows.reshape(owner_count, capacity, features + LANES), "table"
    ).reshape(slots, features + LANES)

    slab = pl.pallas_call(slab_kernel, out_shape=shape((slab_rows, features), bf16), compiler_params=limit(8), name="slab")(
        got_rows
    )
    share = slab_rows // seq_count
    parts = exchange(slab.reshape(seq_count, share, features), "seq")
    copies = pl.pallas_call(
        sum_kernel,
        out_shape=shape((seq_count, share, features), bf16),
        compiler_params=limit(8), name="row_sum",
    )(parts)
    item_grad = exchange(copies, "seq").reshape(slab_rows, features)

    new_table, new_moment, new_second, reply = pl.pallas_call(
        adam_kernel,
        out_shape=(
            shape((slab_rows, features), bf16),
            shape((slab_rows, features), f32),
            shape((slab_rows, 1), f32),
            shape((slots, features), bf16),
        ),
        grid=(1,),
        in_specs=[
            whole((slab_rows, features)),
            whole((slab_rows, features)),
            whole((slab_rows, 1)),
            whole((slab_rows, features)),
            pl.BlockSpec((slots, LANES), lambda i: (0, features // LANES)),
        ],
        out_specs=(
            whole((slab_rows, features)),
            whole((slab_rows, features)),
            whole((slab_rows, 1)),
            whole((slots, features)),
        ),
        compiler_params=limit(12), name="adam",
    )(item_grad, moment, second[:, None], table, got_rows)
    returned = exchange(reply.reshape(owner_count, capacity, features), "table")
    event_rows = pl.pallas_call(
        event_kernel,
        out_shape=shape((tokens, features), bf16),
        compiler_params=limit(8), name="event_rows",
    )(target, returned.reshape(slots, features))
    return (new_table, new_moment, new_second[:, 0], event_rows[None])


def solution(mesh):
    return jax.shard_map(
        body,
        mesh=mesh,
        in_specs=(
            P("table", "seq", None),
            P(),
            P("table", "seq", None),
            P(),
            P("table", "seq"),
            P(),
            P(),
            P("table", None),
            P("table", None),
            P("table"),
        ),
        out_specs=(P("table", None), P("table", None), P("table"), P("table", "seq", None)),
        check_vma=False,
    )
```

```python
import functools
import math

import jax
import jax.numpy as jnp
from jax import lax
from jax.experimental import pallas as pl
from jax.experimental.pallas import tpu as pltpu
from jax.sharding import PartitionSpec as P

HEADS = 8
LANES = 128
DIGIT = 16

first_decay = 0.9
second_decay = 0.99
step_rate = 0.05
epsilon = 1e-08

f32 = jnp.float32
bf16 = jnp.bfloat16


def swap_halves(block):
    half = block.shape[1] // 2
    return pltpu.roll(block, half, 1)


def low_lanes(shape):
    return lax.broadcasted_iota(jnp.int32, shape, 1) < shape[1] // 2


def pair_low(first, second):
    return jnp.where(low_lanes(first.shape), first, swap_halves(second))


def pair_high(first, second):
    return jnp.where(low_lanes(first.shape), swap_halves(first), second)


def project_kernel(shift, x_hbm, proj_hbm, grad_hbm, send_ref, x_s, proj_s, grad_s, sems):
    rows, features = x_s.shape
    count = send_ref.shape[0]
    half = rows // 2
    pairs = HEADS // 2
    loads = [pltpu.make_async_copy(x_hbm, x_s, sems.at[pairs])]
    loads.append(pltpu.make_async_copy(grad_hbm, grad_s, sems.at[pairs + 1]))
    for load in loads:
        load.start()
    for third in range(3):
        at = pl.ds(third * features, features)
        loads.append(pltpu.make_async_copy(proj_hbm.at[:, at], proj_s.at[:, at], sems.at[third]))
        loads[-1].start()
    for load in loads:
        load.wait()
    x = x_s[...]
    for pair in range(pairs):
        at = pair * LANES
        queries, keys, values = [
            jnp.dot(
                x, proj_s[:, third * features + at : third * features + at + LANES],
                preferred_element_type=f32,
            )
            for third in range(3)
        ]
        cot = grad_s[:, at : at + LANES].astype(f32)
        for odd, join in ((0, pair_low), (1, pair_high)):
            query_grad = join(queries, cot).astype(bf16)
            key_value = join(keys, values).astype(bf16)
            for part in range(2):
                slot = (2 * (2 * pair + odd) + part - shift) % count
                send_ref[slot, 0:rows, :] = query_grad
                send_ref[slot, rows : rows + half, :] = key_value[part * half : part * half + half]


def attention_kernel(shift, part_ref, seen_ref, got_ref, out_ref, key_s, value_s, total_s):
    blocks = got_ref.shape[0]
    rows = out_ref.shape[1]
    half = rows // 2
    tile = 2 * rows
    history_scale = 1.0 / math.sqrt(rows * blocks)
    part = part_ref[0]
    low = low_lanes((half, LANES))
    for block in range(blocks):
        both = got_ref[(block - shift) % blocks, rows : rows + half, :]
        zero = jnp.zeros_like(both)
        key_s[block * half : block * half + half, :] = jnp.where(
            low, both * jnp.bfloat16(0.0625), zero
        )
        value_s[block * half : block * half + half, :] = jnp.where(low, zero, both)
    key_row = lax.broadcasted_iota(jnp.int32, (rows, tile), 0)
    query_col = lax.broadcasted_iota(jnp.int32, (rows, tile), 1)
    key_pos = (key_row // half) * rows + part * half + key_row % half
    causal = (key_pos <= query_col).astype(f32)
    for step in range(blocks // 2):
        first = step * rows
        count = first + rows
        place = (2 * step - shift) % blocks
        query_grad = got_ref[place : place + 2, 0:rows, :].reshape(tile, LANES)
        keys = key_s[0:count, :]
        half_scores = lax.dot_general(
            keys, query_grad, (((1,), (1,)), ((), ())), preferred_element_type=f32
        )
        weight_grad = lax.dot_general(
            value_s[0:count, :], query_grad, (((1,), (1,)), ((), ())), preferred_element_type=f32
        )
        seen = [
            jnp.broadcast_to(
                seen_ref[block : block + 1, step * tile : step * tile + tile], (half, tile)
            )
            for block in range(2 * step + 2)
        ]
        for b in range(2):
            seen[2 * step + b] = seen[2 * step + b] * causal[b * half : b * half + half]
        gate2 = (1.0 + jnp.tanh(half_scores)) * jnp.concatenate(seen, axis=0)
        weights = half_scores * gate2
        score_grad = (weight_grad * (gate2 + weights * (2.0 - gate2))).astype(bf16)
        weights = weights.astype(bf16)
        key_part = jnp.dot(score_grad, query_grad, preferred_element_type=f32)
        value_part = jnp.dot(weights, query_grad, preferred_element_type=f32)
        joined = jnp.where(low_lanes(key_part.shape), key_part, value_part)
        if step > 0:
            total_s[0:first, :] += joined[0:first]
        total_s[first:count, :] = joined[first:count]
        query_total = history_scale * lax.dot_general(
            score_grad, keys, (((0,), (0,)), ((), ())), preferred_element_type=f32
        )
        for b in range(2):
            top = query_total[b * rows : b * rows + half]
            bottom = query_total[b * rows + half : b * rows + rows]
            out_ref[place + b, half:rows, :] = (top + swap_halves(bottom)).astype(bf16)
    scale = jnp.where(low_lanes((1, LANES)), history_scale * 0.0625, history_scale)
    for block in range(blocks):
        out_ref[(block - shift) % blocks, 0:half, :] = (
            total_s[block * half : block * half + half, :] * scale
        ).astype(bf16)


def input_grad_kernel(shift, got_ref, proj_ref, target_ref, digits_ref, send_ref):
    count, rows = got_ref.shape[0:2]
    half = rows // 2
    queries, keys, values = [], [], []
    for pair in range(HEADS // 2):
        query, joint = [], []
        for odd in range(2):
            slot = (2 * (2 * pair + odd) - shift) % count
            query.append(
                got_ref[slot, half:rows, :].astype(f32) + got_ref[slot + 1, half:rows, :].astype(f32)
            )
            joint.append(
                jnp.concatenate(
                    [got_ref[slot, 0:half, :], got_ref[slot + 1, 0:half, :]], axis=0
                ).astype(f32)
            )
        queries.append(jnp.concatenate([pair_low(*query), pair_high(*query)], axis=0))
        keys.append(pair_low(*joint))
        values.append(pair_high(*joint))
    stacked = jnp.concatenate(queries + keys + values, axis=1).astype(bf16)
    input_grad = lax.dot_general(
        stacked, proj_ref[...], (((1,), (1,)), ((), ())), preferred_element_type=f32
    ).astype(bf16)
    slots = send_ref.shape[0]
    features = input_grad.shape[1]
    onehot = (
        lax.broadcasted_iota(jnp.int32, (slots, rows), 0) == target_ref[...]
    ).astype(f32).astype(bf16)
    send_ref[:, 0:features] = jnp.dot(onehot, input_grad, preferred_element_type=f32).astype(bf16)
    send_ref[:, features:] = jnp.dot(onehot, digits_ref[...], preferred_element_type=f32).astype(bf16)


def slot_rows(digits, slab_rows):
    digits = digits.astype(f32)
    row = digits[:, 0:1] * DIGIT + digits[:, 1:2] - DIGIT
    lane = lax.broadcasted_iota(jnp.int32, (digits.shape[0], slab_rows), 1).astype(f32)
    return (row == lane).astype(f32).astype(bf16)


def slab_kernel(got_ref, slab_ref):
    slab_rows, features = slab_ref.shape
    select = slot_rows(got_ref[:, features:], slab_rows)
    slab_ref[...] = lax.dot_general(
        select, got_ref[:, 0:features], (((0,), (0,)), ((), ())), preferred_element_type=f32
    ).astype(bf16)


def sum_kernel(got_ref, out_ref):
    count = got_ref.shape[0]
    total = got_ref[0].astype(f32)
    for source in range(1, count):
        total += got_ref[source].astype(f32)
    total = total.astype(bf16)
    for target in range(count):
        out_ref[target] = total


def adam_kernel(
    grad_ref, moment_ref, second_ref, table_ref, digits_ref,
    new_table_ref, new_moment_ref, new_second_ref, reply_ref,
):
    item_grad = grad_ref[...].astype(f32)
    new_moment = first_decay * moment_ref[...] + (1.0 - first_decay) * item_grad
    new_moment_ref[...] = new_moment
    mean = jnp.mean(item_grad * item_grad, axis=1, keepdims=True)
    new_second = second_decay * second_ref[...] + (1.0 - second_decay) * mean
    new_second_ref[...] = new_second
    new_table = (
        table_ref[...].astype(f32) - step_rate * new_moment / (jnp.sqrt(new_second) + epsilon)
    ).astype(bf16)
    new_table_ref[...] = new_table
    select = slot_rows(digits_ref[...], new_table.shape[0])
    reply_ref[...] = jnp.dot(select, new_table, preferred_element_type=f32).astype(bf16)


def event_kernel(target_ref, got_ref, out_ref):
    slots = got_ref.shape[0]
    rows = out_ref.shape[0]
    onehot = (
        lax.broadcasted_iota(jnp.int32, (slots, rows), 0) == target_ref[...]
    ).astype(f32).astype(bf16)
    out_ref[...] = lax.dot_general(
        onehot, got_ref[...], (((0,), (0,)), ((), ())), preferred_element_type=f32
    ).astype(bf16)


def limit(mib):
    return pltpu.CompilerParams(vmem_limit_bytes=mib * 1024 * 1024)


def whole(dims):
    return pl.BlockSpec(dims, lambda i: (0, 0))


def shape(dims, kind):
    return jax.ShapeDtypeStruct(dims, kind)


def exchange(array, axis, shift):
    count = array.shape[0]
    order = [[(member + shift) % count for member in range(count)]]
    return lax.all_to_all(
        array, axis, split_axis=0, concat_axis=0, axis_index_groups=order, tiled=True
    )


def body(events_x, proj, out_grad, block_mask, item_ids, owner_of, local_of, table, moment, second):
    tokens = events_x.shape[1]
    features = events_x.shape[2]
    seq_count = lax.axis_size("seq")
    owner_count = lax.axis_size("table")
    position = lax.axis_index("seq")
    slab_rows = table.shape[0]
    capacity = 2 * tokens // owner_count
    slots = owner_count * capacity
    half = tokens // 2
    seq_shift = seq_count // 2 + math.isqrt(seq_count) // 2
    table_shift = owner_count // 2

    in_hbm = pl.BlockSpec(memory_space=pltpu.MemorySpace.HBM)
    send = pl.pallas_call(
        functools.partial(project_kernel, seq_shift),
        out_shape=shape((seq_count, tokens + half, LANES), bf16),
        in_specs=[in_hbm, in_hbm, in_hbm],
        scratch_shapes=[
            pltpu.VMEM((tokens, features), bf16),
            pltpu.VMEM((features, 3 * features), bf16),
            pltpu.VMEM((tokens, features), bf16),
            pltpu.SemaphoreType.DMA((HEADS // 2 + 2,)),
        ],
        compiler_params=limit(60), name="project",
    )(events_x[0], proj, out_grad[0])
    got = exchange(send, "seq", seq_shift)

    block_ids = jnp.arange(seq_count)
    visible = (block_mask == 1) | (block_ids[:, None] == block_ids[None, :])
    seen = jnp.repeat(visible.T.astype(f32), tokens, axis=1)
    part = (position % 2).astype(jnp.int32).reshape(1)
    back = pl.pallas_call(
        functools.partial(attention_kernel, seq_shift),
        out_shape=shape((seq_count, tokens, LANES), bf16),
        in_specs=[
            pl.BlockSpec(memory_space=pltpu.SMEM),
            pl.BlockSpec(memory_space=pltpu.VMEM),
            pl.BlockSpec(memory_space=pltpu.VMEM),
        ],
        scratch_shapes=[
            pltpu.VMEM((seq_count * half, LANES), bf16),
            pltpu.VMEM((seq_count * half, LANES), bf16),
            pltpu.VMEM((seq_count * half, LANES), f32),
        ],
        compiler_params=limit(24), name="attention",
    )(part, seen, got)
    got_back = exchange(back, "seq", seq_shift)

    place_of = owner_of * slab_rows + local_of
    place = place_of[item_ids[0]]
    owners = place // slab_rows
    slab_index = place % slab_rows
    event = jnp.arange(tokens)
    earlier = (owners[:, None] == owners[None, :]) & (event[:, None] < event[None, :])
    rank = jnp.sum(earlier.astype(jnp.int32), axis=0)
    member = (owners - table_shift) % owner_count
    target = (member * capacity + rank)[None, :]
    lane = jnp.arange(LANES)[None, :]
    digits = jnp.where(
        lane == 0,
        (slab_index // DIGIT + 1)[:, None],
        jnp.where(lane == 1, (slab_index % DIGIT)[:, None], 0),
    ).astype(bf16)
    send_rows = pl.pallas_call(
        functools.partial(input_grad_kernel, seq_shift),
        out_shape=shape((slots, features + LANES), bf16),
        compiler_params=limit(12), name="input_grad",
    )(got_back, proj, target, digits)
    got_rows = exchange(
        send_rows.reshape(owner_count, capacity, features + LANES), "table", table_shift
    ).reshape(slots, features + LANES)

    slab = pl.pallas_call(slab_kernel, out_shape=shape((slab_rows, features), bf16), compiler_params=limit(8), name="slab")(
        got_rows
    )
    share = slab_rows // seq_count
    parts = exchange(slab.reshape(seq_count, share, features), "seq", seq_shift)
    copies = pl.pallas_call(
        sum_kernel,
        out_shape=shape((seq_count, share, features), bf16),
        compiler_params=limit(8), name="row_sum",
    )(parts)
    item_grad = exchange(copies, "seq", seq_shift).reshape(slab_rows, features)

    new_table, new_moment, new_second, reply = pl.pallas_call(
        adam_kernel,
        out_shape=(
            shape((slab_rows, features), bf16),
            shape((slab_rows, features), f32),
            shape((slab_rows, 1), f32),
            shape((slots, features), bf16),
        ),
        grid=(1,),
        in_specs=[
            whole((slab_rows, features)),
            whole((slab_rows, features)),
            whole((slab_rows, 1)),
            whole((slab_rows, features)),
            pl.BlockSpec((slots, LANES), lambda i: (0, features // LANES)),
        ],
        out_specs=(
            whole((slab_rows, features)),
            whole((slab_rows, features)),
            whole((slab_rows, 1)),
            whole((slots, features)),
        ),
        compiler_params=limit(12), name="adam",
    )(item_grad, moment, second[:, None], table, got_rows)
    returned = exchange(reply.reshape(owner_count, capacity, features), "table", table_shift)
    event_rows = pl.pallas_call(
        event_kernel,
        out_shape=shape((tokens, features), bf16),
        compiler_params=limit(8), name="event_rows",
    )(target, returned.reshape(slots, features))
    return (new_table, new_moment, new_second[:, 0], event_rows[None])


def solution(mesh):
    return jax.shard_map(
        body,
        mesh=mesh,
        in_specs=(
            P("table", "seq", None),
            P(),
            P("table", "seq", None),
            P(),
            P("table", "seq"),
            P(),
            P(),
            P("table", None),
            P("table", None),
            P("table"),
        ),
        out_specs=(P("table", None), P("table", None), P("table"), P("table", "seq", None)),
        check_vma=False,
    )
```

```python
import functools
import math

import jax
import jax.numpy as jnp
from jax import lax
from jax.experimental import pallas as pl
from jax.experimental.pallas import tpu as pltpu
from jax.sharding import PartitionSpec as P

HEADS = 8
LANES = 128
DIGIT = 16

first_decay = 0.9
second_decay = 0.99
step_rate = 0.05
epsilon = 1e-08

f32 = jnp.float32
bf16 = jnp.bfloat16


def swap_halves(block):
    half = block.shape[1] // 2
    return pltpu.roll(block, half, 1)


def low_lanes(shape):
    return lax.broadcasted_iota(jnp.int32, shape, 1) < shape[1] // 2


def pair_low(first, second):
    return jnp.where(low_lanes(first.shape), first, swap_halves(second))


def pair_high(first, second):
    return jnp.where(low_lanes(first.shape), swap_halves(first), second)


def project_kernel(shift, x_ref, proj_ref, grad_ref, send_ref):
    features = x_ref.shape[1]
    rows = x_ref.shape[0]
    half = rows // 2
    count = send_ref.shape[0]
    x = x_ref[...]
    for pair in range(HEADS // 2):
        at = pair * LANES
        parts = [
            jnp.dot(
                x, proj_ref[:, third * features + at : third * features + at + LANES],
                preferred_element_type=f32,
            )
            for third in range(3)
        ]
        cot = grad_ref[:, at : at + LANES].astype(f32)
        queries, keys, values = parts
        for odd, join in ((0, pair_low), (1, pair_high)):
            query_grad = join(queries, cot).astype(bf16)
            key_value = join(keys, values).astype(bf16)
            for part in range(2):
                slot = (2 * (2 * pair + odd) + part - shift) % count
                send_ref[slot, 0:rows, :] = query_grad
                send_ref[slot, rows : rows + half, :] = key_value[part * half : part * half + half]


def attention_kernel(shift, part_ref, seen_ref, got_ref, out_ref, key_s, value_s, total_s, key_t):
    blocks = got_ref.shape[0]
    rows = out_ref.shape[1]
    half = rows // 2
    tile = 2 * rows
    history_scale = 1.0 / math.sqrt(rows * blocks)
    part = part_ref[0]
    low = low_lanes((half, LANES))
    for block in range(blocks):
        both = got_ref[(block - shift) % blocks, rows : rows + half, :]
        zero = jnp.zeros_like(both)
        key_s[block * half : block * half + half, :] = jnp.where(
            low, both * jnp.bfloat16(0.0625), zero
        )
        value_s[block * half : block * half + half, :] = jnp.where(low, zero, both)
    key_t[...] = key_s[...].astype(f32).T[0:half].astype(bf16)
    key_row = lax.broadcasted_iota(jnp.int32, (rows, tile), 0)
    query_col = lax.broadcasted_iota(jnp.int32, (rows, tile), 1)
    key_pos = (key_row // half) * rows + part * half + key_row % half
    causal = (key_pos <= query_col).astype(f32)
    for step in range(blocks // 2):
        first = step * rows
        count = first + rows
        place = (2 * step - shift) % blocks
        query_grad = got_ref[place : place + 2, 0:rows, :].reshape(tile, LANES)
        keys = key_s[0:count, :]
        half_scores = lax.dot_general(
            keys, query_grad, (((1,), (1,)), ((), ())), preferred_element_type=f32
        )
        weight_grad = lax.dot_general(
            value_s[0:count, :], query_grad, (((1,), (1,)), ((), ())), preferred_element_type=f32
        )
        seen = [
            jnp.broadcast_to(
                seen_ref[block : block + 1, step * tile : step * tile + tile], (half, tile)
            )
            for block in range(2 * step + 2)
        ]
        for b in range(2):
            seen[2 * step + b] = seen[2 * step + b] * causal[b * half : b * half + half]
        gate2 = (1.0 + jnp.tanh(half_scores)) * jnp.concatenate(seen, axis=0)
        weights = half_scores * gate2
        score_grad = (weight_grad * (gate2 + weights * (2.0 - gate2))).astype(bf16)
        weights = weights.astype(bf16)
        key_part = jnp.dot(score_grad, query_grad, preferred_element_type=f32)
        value_part = jnp.dot(weights, query_grad, preferred_element_type=f32)
        joined = jnp.where(low_lanes(key_part.shape), key_part, value_part)
        if step > 0:
            total_s[0:first, :] += joined[0:first]
        total_s[first:count, :] = joined[first:count]
        query_total = history_scale * jnp.dot(
            key_t[:, 0:count], score_grad, preferred_element_type=f32
        )
        for b in range(2):
            top = query_total[:, b * rows : b * rows + half]
            bottom = query_total[:, b * rows + half : b * rows + rows]
            out_ref[place + b, half:rows, :] = (
                jnp.concatenate([top, bottom], axis=0).T.astype(bf16)
            )
    scale = jnp.where(low_lanes((1, LANES)), history_scale * 0.0625, history_scale)
    for block in range(blocks):
        out_ref[(block - shift) % blocks, 0:half, :] = (
            total_s[block * half : block * half + half, :] * scale
        ).astype(bf16)


def input_grad_kernel(shift, got_ref, proj_ref, target_ref, digits_ref, send_ref):
    count, rows = got_ref.shape[0:2]
    half = rows // 2
    queries, keys, values = [], [], []
    for pair in range(HEADS // 2):
        query, joint = [], []
        for odd in range(2):
            slot = (2 * (2 * pair + odd) - shift) % count
            query.append(
                got_ref[slot, half:rows, :].astype(f32) + got_ref[slot + 1, half:rows, :].astype(f32)
            )
            joint.append(
                jnp.concatenate(
                    [got_ref[slot, 0:half, :], got_ref[slot + 1, 0:half, :]], axis=0
                ).astype(f32)
            )
        queries.append(jnp.concatenate([pair_low(*query), pair_high(*query)], axis=0))
        keys.append(pair_low(*joint))
        values.append(pair_high(*joint))
    stacked = jnp.concatenate(queries + keys + values, axis=1).astype(bf16)
    input_grad = lax.dot_general(
        stacked, proj_ref[...], (((1,), (1,)), ((), ())), preferred_element_type=f32
    ).astype(bf16)
    slots = send_ref.shape[0]
    features = input_grad.shape[1]
    onehot = (
        lax.broadcasted_iota(jnp.int32, (slots, rows), 0) == target_ref[...]
    ).astype(f32).astype(bf16)
    send_ref[:, 0:features] = jnp.dot(onehot, input_grad, preferred_element_type=f32).astype(bf16)
    send_ref[:, features:] = jnp.dot(onehot, digits_ref[...], preferred_element_type=f32).astype(bf16)


def slot_rows(digits, slab_rows):
    digits = digits.astype(f32)
    row = digits[:, 0:1] * DIGIT + digits[:, 1:2] - DIGIT
    lane = lax.broadcasted_iota(jnp.int32, (digits.shape[0], slab_rows), 1).astype(f32)
    return (row == lane).astype(f32).astype(bf16)


def slab_kernel(got_ref, slab_ref):
    slab_rows, features = slab_ref.shape
    select = slot_rows(got_ref[:, features:], slab_rows)
    slab_ref[...] = lax.dot_general(
        select, got_ref[:, 0:features], (((0,), (0,)), ((), ())), preferred_element_type=f32
    ).astype(bf16)


def sum_kernel(got_ref, out_ref):
    count = got_ref.shape[0]
    total = got_ref[0].astype(f32)
    for source in range(1, count):
        total += got_ref[source].astype(f32)
    total = total.astype(bf16)
    for target in range(count):
        out_ref[target] = total


def adam_kernel(
    grad_ref, moment_ref, second_ref, table_ref, digits_ref, new_table_ref, new_second_ref, reply_ref
):
    item_grad = grad_ref[...].astype(f32)
    mean = jnp.mean(item_grad * item_grad, axis=1, keepdims=True)
    new_second = second_decay * second_ref[...] + (1.0 - second_decay) * mean
    new_second_ref[...] = new_second
    rate = step_rate / (jnp.sqrt(new_second) + epsilon)
    new_moment = first_decay * moment_ref[...] + (1.0 - first_decay) * item_grad
    new_table = (table_ref[...].astype(f32) - new_moment * rate).astype(bf16)
    new_table_ref[...] = new_table
    select = slot_rows(digits_ref[...], new_table.shape[0])
    reply_ref[...] = jnp.dot(select, new_table, preferred_element_type=f32).astype(bf16)


def event_kernel(target_ref, got_ref, out_ref):
    slots = got_ref.shape[0]
    rows = out_ref.shape[0]
    onehot = (
        lax.broadcasted_iota(jnp.int32, (slots, rows), 0) == target_ref[...]
    ).astype(f32).astype(bf16)
    out_ref[...] = lax.dot_general(
        onehot, got_ref[...], (((0,), (0,)), ((), ())), preferred_element_type=f32
    ).astype(bf16)


def limit(mib):
    return pltpu.CompilerParams(vmem_limit_bytes=mib * 1024 * 1024)


def whole(dims):
    return pl.BlockSpec(dims, lambda i: (0, 0))


def shape(dims, kind):
    return jax.ShapeDtypeStruct(dims, kind)


def exchange(array, axis, shift):
    count = array.shape[0]
    order = [[(member + shift) % count for member in range(count)]]
    return lax.all_to_all(
        array, axis, split_axis=0, concat_axis=0, axis_index_groups=order, tiled=True
    )


def body(events_x, proj, out_grad, block_mask, item_ids, owner_of, local_of, table, moment, second):
    tokens = events_x.shape[1]
    features = events_x.shape[2]
    seq_count = lax.axis_size("seq")
    owner_count = lax.axis_size("table")
    position = lax.axis_index("seq")
    slab_rows = table.shape[0]
    capacity = 2 * tokens // owner_count
    slots = owner_count * capacity
    half = tokens // 2
    seq_shift = seq_count // 2 + math.isqrt(seq_count) // 2
    table_shift = owner_count // 2 + 2

    send = pl.pallas_call(
        functools.partial(project_kernel, seq_shift),
        out_shape=shape((seq_count, tokens + half, LANES), bf16),
        compiler_params=limit(60), name="project",
    )(events_x[0], proj, out_grad[0])
    got = exchange(send, "seq", seq_shift)

    block_ids = jnp.arange(seq_count)
    visible = (block_mask == 1) | (block_ids[:, None] == block_ids[None, :])
    seen = jnp.repeat(visible.T.astype(f32), tokens, axis=1)
    part = (position % 2).astype(jnp.int32).reshape(1)
    back = pl.pallas_call(
        functools.partial(attention_kernel, seq_shift),
        out_shape=shape((seq_count, tokens, LANES), bf16),
        in_specs=[
            pl.BlockSpec(memory_space=pltpu.SMEM),
            pl.BlockSpec(memory_space=pltpu.VMEM),
            pl.BlockSpec(memory_space=pltpu.VMEM),
        ],
        scratch_shapes=[
            pltpu.VMEM((seq_count * half, LANES), bf16),
            pltpu.VMEM((seq_count * half, LANES), bf16),
            pltpu.VMEM((seq_count * half, LANES), f32),
            pltpu.VMEM((half, seq_count * half), bf16),
        ],
        compiler_params=limit(24), name="attention",
    )(part, seen, got)
    got_back = exchange(back, "seq", seq_shift)

    place_of = owner_of * slab_rows + local_of
    place = place_of[item_ids[0]]
    owners = place // slab_rows
    slab_index = place % slab_rows
    event = jnp.arange(tokens)
    earlier = (owners[:, None] == owners[None, :]) & (event[:, None] < event[None, :])
    rank = jnp.sum(earlier.astype(jnp.int32), axis=0)
    member = (owners - table_shift) % owner_count
    target = (member * capacity + rank)[None, :]
    lane = jnp.arange(LANES)[None, :]
    digits = jnp.where(
        lane == 0,
        (slab_index // DIGIT + 1)[:, None],
        jnp.where(lane == 1, (slab_index % DIGIT)[:, None], 0),
    ).astype(bf16)
    send_rows = pl.pallas_call(
        functools.partial(input_grad_kernel, seq_shift),
        out_shape=shape((slots, features + LANES), bf16),
        compiler_params=limit(12), name="input_grad",
    )(got_back, proj, target, digits)
    got_rows = exchange(
        send_rows.reshape(owner_count, capacity, features + LANES), "table", table_shift
    ).reshape(slots, features + LANES)

    slab = pl.pallas_call(slab_kernel, out_shape=shape((slab_rows, features), bf16), compiler_params=limit(8), name="slab")(
        got_rows
    )
    share = slab_rows // seq_count
    parts = exchange(slab.reshape(seq_count, share, features), "seq", seq_shift)
    copies = pl.pallas_call(
        sum_kernel,
        out_shape=shape((seq_count, share, features), bf16),
        compiler_params=limit(8), name="row_sum",
    )(parts)
    item_grad = exchange(copies, "seq", seq_shift).reshape(slab_rows, features)

    new_table, new_second, reply = pl.pallas_call(
        adam_kernel,
        out_shape=(
            shape((slab_rows, features), bf16),
            shape((slab_rows, 1), f32),
            shape((slots, features), bf16),
        ),
        grid=(1,),
        in_specs=[
            whole((slab_rows, features)),
            whole((slab_rows, features)),
            whole((slab_rows, 1)),
            whole((slab_rows, features)),
            pl.BlockSpec((slots, LANES), lambda i: (0, features // LANES)),
        ],
        out_specs=(
            whole((slab_rows, features)),
            whole((slab_rows, 1)),
            whole((slots, features)),
        ),
        compiler_params=limit(12), name="adam",
    )(item_grad, moment, second[:, None], table, got_rows)
    new_moment = first_decay * moment + (1.0 - first_decay) * item_grad.astype(f32)
    returned = exchange(reply.reshape(owner_count, capacity, features), "table", table_shift)
    event_rows = pl.pallas_call(
        event_kernel,
        out_shape=shape((tokens, features), bf16),
        compiler_params=limit(8), name="event_rows",
    )(target, returned.reshape(slots, features))
    return (new_table, new_moment, new_second[:, 0], event_rows[None])


def solution(mesh):
    return jax.shard_map(
        body,
        mesh=mesh,
        in_specs=(
            P("table", "seq", None),
            P(),
            P("table", "seq", None),
            P(),
            P("table", "seq"),
            P(),
            P(),
            P("table", None),
            P("table", None),
            P("table"),
        ),
        out_specs=(P("table", None), P("table", None), P("table"), P("table", "seq", None)),
        check_vma=False,
    )
```

```python
import functools
import math

import jax
import jax.numpy as jnp
from jax import lax
from jax.experimental import pallas as pl
from jax.experimental.pallas import tpu as pltpu
from jax.sharding import PartitionSpec as P

HEADS = 8
LANES = 128
DIGIT = 16

first_decay = 0.9
second_decay = 0.99
step_rate = 0.05
epsilon = 1e-08

f32 = jnp.float32
bf16 = jnp.bfloat16


def swap_halves(block):
    half = block.shape[1] // 2
    return pltpu.roll(block, half, 1)


def low_lanes(shape):
    return lax.broadcasted_iota(jnp.int32, shape, 1) < shape[1] // 2


def pair_low(first, second):
    return jnp.where(low_lanes(first.shape), first, swap_halves(second))


def pair_high(first, second):
    return jnp.where(low_lanes(first.shape), swap_halves(first), second)


def project_kernel(shift, x_ref, proj_ref, grad_ref, send_ref):
    features = x_ref.shape[1]
    rows = x_ref.shape[0]
    half = rows // 2
    count = send_ref.shape[0]
    x = x_ref[...]
    for pair in range(HEADS // 2):
        at = pair * LANES
        parts = [
            jnp.dot(
                x, proj_ref[:, third * features + at : third * features + at + LANES],
                preferred_element_type=f32,
            )
            for third in range(3)
        ]
        cot = grad_ref[:, at : at + LANES].astype(f32)
        queries, keys, values = parts
        for odd, join in ((0, pair_low), (1, pair_high)):
            query_grad = join(queries, cot).astype(bf16)
            key_value = join(keys, values).astype(bf16)
            for part in range(2):
                slot = (2 * (2 * pair + odd) + part - shift) % count
                send_ref[slot, 0:rows, :] = query_grad
                send_ref[slot, rows : rows + half, :] = key_value[part * half : part * half + half]


def attention_kernel(shift, part_ref, seen_ref, got_ref, out_ref, key_s, value_s, total_s, key_t):
    blocks = got_ref.shape[0]
    rows = out_ref.shape[1]
    half = rows // 2
    tile = 2 * rows
    history_scale = 1.0 / math.sqrt(rows * blocks)
    part = part_ref[0]
    low = low_lanes((half, LANES))
    for block in range(blocks):
        both = got_ref[(block - shift) % blocks, rows : rows + half, :]
        zero = jnp.zeros_like(both)
        key_s[block * half : block * half + half, :] = jnp.where(
            low, both * jnp.bfloat16(0.0625), zero
        )
        value_s[block * half : block * half + half, :] = jnp.where(low, zero, both)
    key_t[...] = key_s[...].astype(f32).T[0:half].astype(bf16)
    key_row = lax.broadcasted_iota(jnp.int32, (rows, tile), 0)
    query_col = lax.broadcasted_iota(jnp.int32, (rows, tile), 1)
    key_pos = (key_row // half) * rows + part * half + key_row % half
    causal = (key_pos <= query_col).astype(f32)
    for step in range(blocks // 2):
        first = step * rows
        count = first + rows
        place = (2 * step - shift) % blocks
        query_grad = got_ref[place : place + 2, 0:rows, :].reshape(tile, LANES)
        keys = key_s[0:count, :]
        half_scores = lax.dot_general(
            keys, query_grad, (((1,), (1,)), ((), ())), preferred_element_type=f32
        )
        weight_grad = lax.dot_general(
            value_s[0:count, :], query_grad, (((1,), (1,)), ((), ())), preferred_element_type=f32
        )
        seen = [
            jnp.broadcast_to(
                seen_ref[block : block + 1, step * tile : step * tile + tile], (half, tile)
            )
            for block in range(2 * step + 2)
        ]
        for b in range(2):
            seen[2 * step + b] = seen[2 * step + b] * causal[b * half : b * half + half]
        gate2 = (1.0 + jnp.tanh(half_scores)) * jnp.concatenate(seen, axis=0)
        weights = half_scores * gate2
        score_grad = (weight_grad * (gate2 + weights * (2.0 - gate2))).astype(bf16)
        weights = weights.astype(bf16)
        key_part = jnp.dot(score_grad, query_grad, preferred_element_type=f32)
        value_part = jnp.dot(weights, query_grad, preferred_element_type=f32)
        joined = jnp.where(low_lanes(key_part.shape), key_part, value_part)
        if step > 0:
            total_s[0:first, :] += joined[0:first]
        total_s[first:count, :] = joined[first:count]
        query_total = history_scale * jnp.dot(
            key_t[:, 0:count], score_grad, preferred_element_type=f32
        )
        for b in range(2):
            top = query_total[:, b * rows : b * rows + half]
            bottom = query_total[:, b * rows + half : b * rows + rows]
            out_ref[place + b, half:rows, :] = (
                jnp.concatenate([top, bottom], axis=0).T.astype(bf16)
            )
    scale = jnp.where(low_lanes((1, LANES)), history_scale * 0.0625, history_scale)
    for block in range(blocks):
        out_ref[(block - shift) % blocks, 0:half, :] = (
            total_s[block * half : block * half + half, :] * scale
        ).astype(bf16)


def input_grad_kernel(shift, got_ref, proj_ref, target_ref, digits_ref, send_ref):
    count, rows = got_ref.shape[0:2]
    half = rows // 2
    queries, keys, values = [], [], []
    for pair in range(HEADS // 2):
        query, joint = [], []
        for odd in range(2):
            slot = (2 * (2 * pair + odd) - shift) % count
            query.append(
                got_ref[slot, half:rows, :].astype(f32) + got_ref[slot + 1, half:rows, :].astype(f32)
            )
            joint.append(
                jnp.concatenate(
                    [got_ref[slot, 0:half, :], got_ref[slot + 1, 0:half, :]], axis=0
                ).astype(f32)
            )
        queries.append(jnp.concatenate([pair_low(*query), pair_high(*query)], axis=0))
        keys.append(pair_low(*joint))
        values.append(pair_high(*joint))
    stacked = jnp.concatenate(queries + keys + values, axis=1).astype(bf16)
    input_grad = lax.dot_general(
        stacked, proj_ref[...], (((1,), (1,)), ((), ())), preferred_element_type=f32
    ).astype(bf16)
    slots = send_ref.shape[0]
    features = input_grad.shape[1]
    onehot = (
        lax.broadcasted_iota(jnp.int32, (slots, rows), 0) == target_ref[...]
    ).astype(f32).astype(bf16)
    send_ref[:, 0:features] = jnp.dot(onehot, input_grad, preferred_element_type=f32).astype(bf16)
    send_ref[:, features:] = jnp.dot(onehot, digits_ref[...], preferred_element_type=f32).astype(bf16)


def slot_rows(digits, slab_rows):
    digits = digits.astype(f32)
    row = digits[:, 0:1] * DIGIT + digits[:, 1:2] - DIGIT
    lane = lax.broadcasted_iota(jnp.int32, (digits.shape[0], slab_rows), 1).astype(f32)
    return (row == lane).astype(f32).astype(bf16)


def slab_kernel(got_ref, slab_ref):
    slab_rows, features = slab_ref.shape
    select = slot_rows(got_ref[:, features:], slab_rows)
    slab_ref[...] = lax.dot_general(
        select, got_ref[:, 0:features], (((0,), (0,)), ((), ())), preferred_element_type=f32
    ).astype(bf16)


def sum_kernel(got_ref, out_ref):
    count = got_ref.shape[0]
    total = got_ref[0].astype(f32)
    for source in range(1, count):
        total += got_ref[source].astype(f32)
    total = total.astype(bf16)
    for target in range(count):
        out_ref[target] = total


def adam_kernel(
    grad_ref, moment_ref, second_ref, table_ref, digits_ref, new_table_ref, new_second_ref, reply_ref
):
    item_grad = grad_ref[...].astype(f32)
    mean = jnp.mean(item_grad * item_grad, axis=1, keepdims=True)
    new_second = second_decay * second_ref[:, 0:1] + (1.0 - second_decay) * mean
    new_second_ref[...] = new_second
    rate = step_rate / (jnp.sqrt(new_second) + epsilon)
    new_moment = first_decay * moment_ref[...] + (1.0 - first_decay) * item_grad
    new_table = (table_ref[...].astype(f32) - new_moment * rate).astype(bf16)
    new_table_ref[...] = new_table
    select = slot_rows(digits_ref[...], new_table.shape[0])
    reply_ref[...] = jnp.dot(select, new_table, preferred_element_type=f32).astype(bf16)


def event_kernel(target_ref, got_ref, out_ref):
    slots = got_ref.shape[0]
    rows = out_ref.shape[0]
    onehot = (
        lax.broadcasted_iota(jnp.int32, (slots, rows), 0) == target_ref[...]
    ).astype(f32).astype(bf16)
    out_ref[...] = lax.dot_general(
        onehot, got_ref[...], (((0,), (0,)), ((), ())), preferred_element_type=f32
    ).astype(bf16)


def limit(mib):
    return pltpu.CompilerParams(vmem_limit_bytes=mib * 1024 * 1024)


def whole(dims):
    return pl.BlockSpec(dims, lambda i: (0, 0))


def shape(dims, kind):
    return jax.ShapeDtypeStruct(dims, kind)


def exchange(array, axis, shift):
    count = array.shape[0]
    order = [[(member + shift) % count for member in range(count)]]
    return lax.all_to_all(
        array, axis, split_axis=0, concat_axis=0, axis_index_groups=order, tiled=True
    )


def body(events_x, proj, out_grad, block_mask, item_ids, owner_of, local_of, table, moment, second):
    tokens = events_x.shape[1]
    features = events_x.shape[2]
    seq_count = lax.axis_size("seq")
    owner_count = lax.axis_size("table")
    position = lax.axis_index("seq")
    slab_rows = table.shape[0]
    capacity = 2 * tokens // owner_count
    slots = owner_count * capacity
    half = tokens // 2
    seq_shift = seq_count // 2 + math.isqrt(seq_count) // 2
    table_shift = owner_count // 2 + 2

    send = pl.pallas_call(
        functools.partial(project_kernel, seq_shift),
        out_shape=shape((seq_count, tokens + half, LANES), bf16),
        compiler_params=limit(60), name="project",
    )(events_x[0], proj, out_grad[0])
    got = exchange(send, "seq", seq_shift)

    place_of = owner_of * slab_rows + local_of
    place = place_of[item_ids[0]]
    owners = place // slab_rows
    slab_index = place % slab_rows
    event = jnp.arange(tokens)
    earlier = (owners[:, None] == owners[None, :]) & (event[:, None] < event[None, :])
    rank = jnp.sum(earlier.astype(jnp.int32), axis=0)
    member = (owners - table_shift) % owner_count
    target = (member * capacity + rank)[None, :]
    lane = jnp.arange(LANES)[None, :]
    digits = jnp.where(
        lane == 0,
        (slab_index // DIGIT + 1)[:, None],
        jnp.where(lane == 1, (slab_index % DIGIT)[:, None], 0),
    ).astype(bf16)
    second_col = jnp.broadcast_to(second[:, None], (slab_rows, LANES))
    got, target, digits, second_col = lax.optimization_barrier((got, target, digits, second_col))
    block_ids = jnp.arange(seq_count)
    visible = (block_mask == 1) | (block_ids[:, None] == block_ids[None, :])
    seen = jnp.repeat(visible.T.astype(f32), tokens, axis=1)
    part = (position % 2).astype(jnp.int32).reshape(1)
    back = pl.pallas_call(
        functools.partial(attention_kernel, seq_shift),
        out_shape=shape((seq_count, tokens, LANES), bf16),
        in_specs=[
            pl.BlockSpec(memory_space=pltpu.SMEM),
            pl.BlockSpec(memory_space=pltpu.VMEM),
            pl.BlockSpec(memory_space=pltpu.VMEM),
        ],
        scratch_shapes=[
            pltpu.VMEM((seq_count * half, LANES), bf16),
            pltpu.VMEM((seq_count * half, LANES), bf16),
            pltpu.VMEM((seq_count * half, LANES), f32),
            pltpu.VMEM((half, seq_count * half), bf16),
        ],
        compiler_params=limit(24), name="attention",
    )(part, seen, got)
    got_back = exchange(back, "seq", seq_shift)

    send_rows = pl.pallas_call(
        functools.partial(input_grad_kernel, seq_shift),
        out_shape=shape((slots, features + LANES), bf16),
        compiler_params=limit(12), name="input_grad",
    )(got_back, proj, target, digits)
    got_rows = exchange(
        send_rows.reshape(owner_count, capacity, features + LANES), "table", table_shift
    ).reshape(slots, features + LANES)

    slab = pl.pallas_call(slab_kernel, out_shape=shape((slab_rows, features), bf16), compiler_params=limit(8), name="slab")(
        got_rows
    )
    share = slab_rows // seq_count
    parts = exchange(slab.reshape(seq_count, share, features), "seq", seq_shift)
    copies = pl.pallas_call(
        sum_kernel,
        out_shape=shape((seq_count, share, features), bf16),
        compiler_params=limit(8), name="row_sum",
    )(parts)
    item_grad = exchange(copies, "seq", seq_shift).reshape(slab_rows, features)

    new_table, new_second, reply = pl.pallas_call(
        adam_kernel,
        out_shape=(
            shape((slab_rows, features), bf16),
            shape((slab_rows, 1), f32),
            shape((slots, features), bf16),
        ),
        grid=(1,),
        in_specs=[
            whole((slab_rows, features)),
            whole((slab_rows, features)),
            whole((slab_rows, LANES)),
            whole((slab_rows, features)),
            pl.BlockSpec((slots, LANES), lambda i: (0, features // LANES)),
        ],
        out_specs=(
            whole((slab_rows, features)),
            whole((slab_rows, 1)),
            whole((slots, features)),
        ),
        compiler_params=limit(12), name="adam",
    )(item_grad, moment, second_col, table, got_rows)
    new_moment = first_decay * moment + (1.0 - first_decay) * item_grad.astype(f32)
    returned = exchange(reply.reshape(owner_count, capacity, features), "table", table_shift)
    event_rows = pl.pallas_call(
        event_kernel,
        out_shape=shape((tokens, features), bf16),
        compiler_params=limit(8), name="event_rows",
    )(target, returned.reshape(slots, features))
    return (new_table, new_moment, new_second[:, 0], event_rows[None])


def solution(mesh):
    return jax.shard_map(
        body,
        mesh=mesh,
        in_specs=(
            P("table", "seq", None),
            P(),
            P("table", "seq", None),
            P(),
            P("table", "seq"),
            P(),
            P(),
            P("table", None),
            P("table", None),
            P("table"),
        ),
        out_specs=(P("table", None), P("table", None), P("table"), P("table", "seq", None)),
        check_vma=False,
    )
```

```python
import functools
import math

import jax
import jax.numpy as jnp
from jax import lax
from jax.experimental import pallas as pl
from jax.experimental.pallas import tpu as pltpu
from jax.sharding import PartitionSpec as P

HEADS = 8
LANES = 128
DIGIT = 16

first_decay = 0.9
second_decay = 0.99
step_rate = 0.05
epsilon = 1e-08

f32 = jnp.float32
bf16 = jnp.bfloat16


def swap_halves(block):
    half = block.shape[1] // 2
    return pltpu.roll(block, half, 1)


def low_lanes(shape):
    return lax.broadcasted_iota(jnp.int32, shape, 1) < shape[1] // 2


def pair_low(first, second):
    return jnp.where(low_lanes(first.shape), first, swap_halves(second))


def pair_high(first, second):
    return jnp.where(low_lanes(first.shape), swap_halves(first), second)


def project_kernel(shift, x_ref, proj_ref, grad_ref, send_ref):
    features = x_ref.shape[1]
    rows = x_ref.shape[0]
    half = rows // 2
    count = send_ref.shape[0]
    x = x_ref[...]
    for pair in range(HEADS // 2):
        at = pair * LANES
        parts = [
            jnp.dot(
                x, proj_ref[:, third * features + at : third * features + at + LANES],
                preferred_element_type=f32,
            )
            for third in range(3)
        ]
        cot = grad_ref[:, at : at + LANES].astype(f32)
        queries, keys, values = parts
        for odd, join in ((0, pair_low), (1, pair_high)):
            query_grad = join(queries, cot).astype(bf16)
            key_value = join(keys, values).astype(bf16)
            for part in range(2):
                slot = (2 * (2 * pair + odd) + part - shift) % count
                send_ref[slot, 0:rows, :] = query_grad
                send_ref[slot, rows : rows + half, :] = key_value[part * half : part * half + half]


def attention_kernel(shift, part_ref, seen_ref, got_ref, out_ref, key_s, value_s, total_s, key_t):
    blocks = got_ref.shape[0]
    rows = out_ref.shape[1]
    half = rows // 2
    tile = 2 * rows
    history_scale = 1.0 / math.sqrt(rows * blocks)
    part = part_ref[0]
    low = low_lanes((half, LANES))
    for block in range(blocks):
        both = got_ref[(block - shift) % blocks, rows : rows + half, :]
        zero = jnp.zeros_like(both)
        key_s[block * half : block * half + half, :] = jnp.where(
            low, both * jnp.bfloat16(0.0625), zero
        )
        value_s[block * half : block * half + half, :] = jnp.where(low, zero, both)
    key_t[...] = key_s[...].astype(f32).T[0:half].astype(bf16)
    key_row = lax.broadcasted_iota(jnp.int32, (rows, tile), 0)
    query_col = lax.broadcasted_iota(jnp.int32, (rows, tile), 1)
    key_pos = (key_row // half) * rows + part * half + key_row % half
    causal = (key_pos <= query_col).astype(f32)
    for step in range(blocks // 2):
        first = step * rows
        count = first + rows
        place = (2 * step - shift) % blocks
        query_grad = got_ref[place : place + 2, 0:rows, :].reshape(tile, LANES)
        keys = key_s[0:count, :]
        half_scores = lax.dot_general(
            keys, query_grad, (((1,), (1,)), ((), ())), preferred_element_type=f32
        )
        weight_grad = lax.dot_general(
            value_s[0:count, :], query_grad, (((1,), (1,)), ((), ())), preferred_element_type=f32
        )
        seen = [
            jnp.broadcast_to(
                seen_ref[block : block + 1, step * tile : step * tile + tile], (half, tile)
            )
            for block in range(2 * step + 2)
        ]
        for b in range(2):
            seen[2 * step + b] = seen[2 * step + b] * causal[b * half : b * half + half]
        gate2 = (1.0 + jnp.tanh(half_scores)) * jnp.concatenate(seen, axis=0)
        weights = half_scores * gate2
        score_grad = (weight_grad * (gate2 + weights * (2.0 - gate2))).astype(bf16)
        weights = weights.astype(bf16)
        key_part = jnp.dot(score_grad, query_grad, preferred_element_type=f32)
        value_part = jnp.dot(weights, query_grad, preferred_element_type=f32)
        joined = jnp.where(low_lanes(key_part.shape), key_part, value_part)
        if step > 0:
            total_s[0:first, :] += joined[0:first]
        total_s[first:count, :] = joined[first:count]
        query_total = history_scale * jnp.dot(
            key_t[:, 0:count], score_grad, preferred_element_type=f32
        )
        for b in range(2):
            top = query_total[:, b * rows : b * rows + half]
            bottom = query_total[:, b * rows + half : b * rows + rows]
            out_ref[place + b, half:rows, :] = (
                jnp.concatenate([top, bottom], axis=0).T.astype(bf16)
            )
    scale = jnp.where(low_lanes((1, LANES)), history_scale * 0.0625, history_scale)
    for block in range(blocks):
        out_ref[(block - shift) % blocks, 0:half, :] = (
            total_s[block * half : block * half + half, :] * scale
        ).astype(bf16)


def input_grad_kernel(shift, got_ref, proj_ref, target_ref, quarter_ref, digits_ref, send_ref):
    count, rows = got_ref.shape[0:2]
    half = rows // 2
    queries, keys, values = [], [], []
    for pair in range(HEADS // 2):
        query, joint = [], []
        for odd in range(2):
            slot = (2 * (2 * pair + odd) - shift) % count
            query.append(
                got_ref[slot, half:rows, :].astype(f32) + got_ref[slot + 1, half:rows, :].astype(f32)
            )
            joint.append(
                jnp.concatenate(
                    [got_ref[slot, 0:half, :], got_ref[slot + 1, 0:half, :]], axis=0
                ).astype(f32)
            )
        queries.append(jnp.concatenate([pair_low(*query), pair_high(*query)], axis=0))
        keys.append(pair_low(*joint))
        values.append(pair_high(*joint))
    stacked = jnp.concatenate(queries + keys + values, axis=1).astype(bf16)
    input_grad = lax.dot_general(
        stacked, proj_ref[...], (((1,), (1,)), ((), ())), preferred_element_type=f32
    ).astype(bf16)
    owners, pieces, lines = send_ref.shape[0:3]
    groups = (pieces - 1) * LANES // input_grad.shape[1]
    slots = groups * owners * lines

    def placed(at_ref, places, values):
        onehot = lax.broadcasted_iota(jnp.int32, (places, rows), 0) == at_ref[...]
        return jnp.dot(onehot.astype(f32).astype(bf16), values, preferred_element_type=f32)

    send_rows = placed(target_ref, slots, input_grad).reshape(owners, groups, lines, -1)
    for piece in range(pieces - 1):
        at = piece // groups * LANES
        send_ref[:, piece] = send_rows[:, piece % groups, :, at : at + LANES].astype(bf16)
    digits = placed(quarter_ref, slots // groups, digits_ref[...]).reshape(owners, lines, LANES)
    send_ref[:, pieces - 1] = digits.astype(bf16)


def slot_rows(digits, slab_rows):
    digits = digits.astype(f32)
    row = digits[:, 0:1] * DIGIT + digits[:, 1:2] - DIGIT
    lane = lax.broadcasted_iota(jnp.int32, (digits.shape[0], slab_rows), 1).astype(f32)
    return (row == lane).astype(f32).astype(bf16)


def slab_kernel(got_ref, slab_ref, digits_ref):
    owners, pieces, lines = got_ref.shape[0:3]
    slab_rows, features = slab_ref.shape
    groups = (pieces - 1) * LANES // features
    first = got_ref[:, pieces - 1].astype(f32).reshape(owners * lines, LANES)
    spread = [first]
    for group in range(1, groups):
        spread.append(pltpu.roll(first, LANES - 2 * group, 1))
    spread = [digits.reshape(owners, lines, LANES) for digits in spread]
    digits = jnp.concatenate(spread, axis=1).reshape(groups * owners * lines, LANES).astype(bf16)
    digits_ref[...] = digits
    select = slot_rows(digits, slab_rows)
    for column in range(features // LANES):
        parts = [got_ref[:, groups * column + group].astype(f32) for group in range(groups)]
        got = jnp.concatenate(parts, axis=1).reshape(digits.shape).astype(bf16)
        slab_ref[:, column * LANES : column * LANES + LANES] = lax.dot_general(
            select, got, (((0,), (0,)), ((), ())), preferred_element_type=f32
        ).astype(bf16)


def sum_kernel(got_ref, out_ref):
    count = got_ref.shape[0]
    total = got_ref[0].astype(f32)
    for source in range(1, count):
        total += got_ref[source].astype(f32)
    total = total.astype(bf16)
    for target in range(count):
        out_ref[target] = total


def adam_kernel(
    grad_ref, moment_ref, second_ref, table_ref, digits_ref, new_table_ref, new_second_ref, reply_ref
):
    item_grad = grad_ref[...].astype(f32)
    mean = jnp.mean(item_grad * item_grad, axis=1, keepdims=True)
    new_second = second_decay * second_ref[:, 0:1] + (1.0 - second_decay) * mean
    new_second_ref[...] = new_second
    rate = step_rate / (jnp.sqrt(new_second) + epsilon)
    new_moment = first_decay * moment_ref[...] + (1.0 - first_decay) * item_grad
    new_table = (table_ref[...].astype(f32) - new_moment * rate).astype(bf16)
    new_table_ref[...] = new_table
    select = slot_rows(digits_ref[...], new_table.shape[0])
    reply_ref[...] = jnp.dot(select, new_table, preferred_element_type=f32).astype(bf16)


def event_kernel(target_ref, got_ref, out_ref):
    slots = got_ref.shape[0]
    rows = out_ref.shape[0]
    onehot = (
        lax.broadcasted_iota(jnp.int32, (slots, rows), 0) == target_ref[...]
    ).astype(f32).astype(bf16)
    out_ref[...] = lax.dot_general(
        onehot, got_ref[...], (((0,), (0,)), ((), ())), preferred_element_type=f32
    ).astype(bf16)


def limit(mib):
    return pltpu.CompilerParams(vmem_limit_bytes=mib * 1024 * 1024)


def whole(dims):
    return pl.BlockSpec(dims, lambda i: (0, 0))


def shape(dims, kind):
    return jax.ShapeDtypeStruct(dims, kind)


def exchange(array, axis, shift):
    count = array.shape[0]
    order = [[(member + shift) % count for member in range(count)]]
    return lax.all_to_all(
        array, axis, split_axis=0, concat_axis=0, axis_index_groups=order, tiled=True
    )


def body(events_x, proj, out_grad, block_mask, item_ids, owner_of, local_of, table, moment, second):
    tokens = events_x.shape[1]
    features = events_x.shape[2]
    seq_count = lax.axis_size("seq")
    owner_count = lax.axis_size("table")
    position = lax.axis_index("seq")
    slab_rows = table.shape[0]
    capacity = 2 * tokens // owner_count
    slots = owner_count * capacity
    half = tokens // 2
    seq_shift = seq_count // 2 + math.isqrt(seq_count) // 2
    table_shift = owner_count // 2 + 2

    send = pl.pallas_call(
        functools.partial(project_kernel, seq_shift),
        out_shape=shape((seq_count, tokens + half, LANES), bf16),
        compiler_params=limit(60), name="project",
    )(events_x[0], proj, out_grad[0])
    got = exchange(send, "seq", seq_shift)

    place_of = owner_of * slab_rows + local_of
    place = place_of[item_ids[0]]
    owners = place // slab_rows
    slab_index = place % slab_rows
    event = jnp.arange(tokens)
    earlier = (owners[:, None] == owners[None, :]) & (event[:, None] < event[None, :])
    rank = jnp.sum(earlier.astype(jnp.int32), axis=0)
    member = (owners - table_shift) % owner_count
    target = (member * capacity + rank)[None, :]
    groups = 4
    lines = capacity // groups
    quarter = (member * lines + rank % lines)[None, :]
    pieces = groups * (features // LANES) + 1
    first_lane = 2 * (rank // lines)
    lane = jnp.arange(LANES)[None, :]
    digits = jnp.where(
        lane == first_lane[:, None],
        (slab_index // DIGIT + 1)[:, None],
        jnp.where(lane == first_lane[:, None] + 1, (slab_index % DIGIT)[:, None], 0),
    ).astype(bf16)
    second_col = jnp.broadcast_to(second[:, None], (slab_rows, LANES))
    got, target, quarter, digits, second_col = lax.optimization_barrier(
        (got, target, quarter, digits, second_col)
    )
    block_ids = jnp.arange(seq_count)
    visible = (block_mask == 1) | (block_ids[:, None] == block_ids[None, :])
    seen = jnp.repeat(visible.T.astype(f32), tokens, axis=1)
    part = (position % 2).astype(jnp.int32).reshape(1)
    back = pl.pallas_call(
        functools.partial(attention_kernel, seq_shift),
        out_shape=shape((seq_count, tokens, LANES), bf16),
        in_specs=[
            pl.BlockSpec(memory_space=pltpu.SMEM),
            pl.BlockSpec(memory_space=pltpu.VMEM),
            pl.BlockSpec(memory_space=pltpu.VMEM),
        ],
        scratch_shapes=[
            pltpu.VMEM((seq_count * half, LANES), bf16),
            pltpu.VMEM((seq_count * half, LANES), bf16),
            pltpu.VMEM((seq_count * half, LANES), f32),
            pltpu.VMEM((half, seq_count * half), bf16),
        ],
        compiler_params=limit(24), name="attention",
    )(part, seen, got)
    got_back = exchange(back, "seq", seq_shift)

    send_rows = pl.pallas_call(
        functools.partial(input_grad_kernel, seq_shift),
        out_shape=shape((owner_count, pieces, lines, LANES), bf16),
        compiler_params=limit(12), name="input_grad",
    )(got_back, proj, target, quarter, digits)
    got_rows = exchange(send_rows, "table", table_shift)

    slab, got_digits = pl.pallas_call(
        slab_kernel,
        out_shape=(shape((slab_rows, features), bf16), shape((slots, LANES), bf16)),
        compiler_params=limit(8), name="slab",
    )(got_rows)
    share = slab_rows // seq_count
    parts = exchange(slab.reshape(seq_count, share, features), "seq", seq_shift)
    copies = pl.pallas_call(
        sum_kernel,
        out_shape=shape((seq_count, share, features), bf16),
        compiler_params=limit(8), name="row_sum",
    )(parts)
    item_grad = exchange(copies, "seq", seq_shift).reshape(slab_rows, features)

    new_table, new_second, reply = pl.pallas_call(
        adam_kernel,
        out_shape=(
            shape((slab_rows, features), bf16),
            shape((slab_rows, 1), f32),
            shape((slots, features), bf16),
        ),
        grid=(1,),
        in_specs=[
            whole((slab_rows, features)),
            whole((slab_rows, features)),
            whole((slab_rows, LANES)),
            whole((slab_rows, features)),
            whole((slots, LANES)),
        ],
        out_specs=(
            whole((slab_rows, features)),
            whole((slab_rows, 1)),
            whole((slots, features)),
        ),
        compiler_params=limit(12), name="adam",
    )(item_grad, moment, second_col, table, got_digits)
    new_moment = first_decay * moment + (1.0 - first_decay) * item_grad.astype(f32)
    returned = exchange(reply.reshape(owner_count, capacity, features), "table", table_shift)
    event_rows = pl.pallas_call(
        event_kernel,
        out_shape=shape((tokens, features), bf16),
        compiler_params=limit(8), name="event_rows",
    )(target, returned.reshape(slots, features))
    return (new_table, new_moment, new_second[:, 0], event_rows[None])


def solution(mesh):
    return jax.shard_map(
        body,
        mesh=mesh,
        in_specs=(
            P("table", "seq", None),
            P(),
            P("table", "seq", None),
            P(),
            P("table", "seq"),
            P(),
            P(),
            P("table", None),
            P("table", None),
            P("table"),
        ),
        out_specs=(P("table", None), P("table", None), P("table"), P("table", "seq", None)),
        check_vma=False,
    )
```

```python
import functools
import math

import jax
import jax.numpy as jnp
from jax import lax
from jax.experimental import pallas as pl
from jax.experimental.pallas import tpu as pltpu
from jax.sharding import PartitionSpec as P

HEADS = 8
LANES = 128
DIGIT = 16

first_decay = 0.9
second_decay = 0.99
step_rate = 0.05
epsilon = 1e-08

f32 = jnp.float32
bf16 = jnp.bfloat16


def swap_halves(block):
    half = block.shape[1] // 2
    return pltpu.roll(block, half, 1)


def low_lanes(shape):
    return lax.broadcasted_iota(jnp.int32, shape, 1) < shape[1] // 2


def pair_low(first, second):
    return jnp.where(low_lanes(first.shape), first, swap_halves(second))


def pair_high(first, second):
    return jnp.where(low_lanes(first.shape), swap_halves(first), second)


def project_kernel(shift, x_ref, proj_ref, grad_ref, send_ref):
    features = x_ref.shape[1]
    rows = x_ref.shape[0]
    half = rows // 2
    count = send_ref.shape[0]
    x = x_ref[...]
    for pair in range(HEADS // 2):
        at = pair * LANES
        parts = [
            jnp.dot(
                x, proj_ref[:, third * features + at : third * features + at + LANES],
                preferred_element_type=f32,
            )
            for third in range(3)
        ]
        cot = grad_ref[:, at : at + LANES].astype(f32)
        queries, keys, values = parts
        for odd, join in ((0, pair_low), (1, pair_high)):
            query_grad = join(queries, cot).astype(bf16)
            key_value = join(keys, values).astype(bf16)
            for part in range(2):
                slot = (2 * (2 * pair + odd) + part - shift) % count
                send_ref[slot, 0:rows, :] = query_grad
                send_ref[slot, rows : rows + half, :] = key_value[part * half : part * half + half]


def attention_kernel(shift, part_ref, seen_ref, got_ref, out_ref, key_s, value_s, total_s, key_t):
    blocks = got_ref.shape[0]
    rows = out_ref.shape[1]
    half = rows // 2
    tile = 2 * rows
    history_scale = 1.0 / math.sqrt(rows * blocks)
    part = part_ref[0]
    low = low_lanes((half, LANES))
    for block in range(blocks):
        both = got_ref[(block - shift) % blocks, rows : rows + half, :]
        zero = jnp.zeros_like(both)
        key_s[block * half : block * half + half, :] = jnp.where(
            low, both * jnp.bfloat16(0.0625), zero
        )
        value_s[block * half : block * half + half, :] = jnp.where(low, zero, both)
    key_t[...] = key_s[...].astype(f32).T[0:half].astype(bf16)
    key_row = lax.broadcasted_iota(jnp.int32, (rows, tile), 0)
    query_col = lax.broadcasted_iota(jnp.int32, (rows, tile), 1)
    key_pos = (key_row // half) * rows + part * half + key_row % half
    causal = (key_pos <= query_col).astype(f32)
    for step in range(blocks // 2):
        first = step * rows
        count = first + rows
        place = (2 * step - shift) % blocks
        query_grad = got_ref[place : place + 2, 0:rows, :].reshape(tile, LANES)
        keys = key_s[0:count, :]
        half_scores = lax.dot_general(
            keys, query_grad, (((1,), (1,)), ((), ())), preferred_element_type=f32
        )
        weight_grad = lax.dot_general(
            value_s[0:count, :], query_grad, (((1,), (1,)), ((), ())), preferred_element_type=f32
        )
        seen = [
            jnp.broadcast_to(
                seen_ref[block : block + 1, step * tile : step * tile + tile], (half, tile)
            )
            for block in range(2 * step + 2)
        ]
        for b in range(2):
            seen[2 * step + b] = seen[2 * step + b] * causal[b * half : b * half + half]
        gate2 = (1.0 + jnp.tanh(half_scores)) * jnp.concatenate(seen, axis=0)
        weights = half_scores * gate2
        score_grad = (weight_grad * (gate2 + weights * (2.0 - gate2))).astype(bf16)
        weights = weights.astype(bf16)
        key_part = jnp.dot(score_grad, query_grad, preferred_element_type=f32)
        value_part = jnp.dot(weights, query_grad, preferred_element_type=f32)
        joined = jnp.where(low_lanes(key_part.shape), key_part, value_part)
        if step > 0:
            total_s[0:first, :] += joined[0:first]
        total_s[first:count, :] = joined[first:count]
        query_total = history_scale * jnp.dot(
            key_t[:, 0:count], score_grad, preferred_element_type=f32
        )
        for b in range(2):
            top = query_total[:, b * rows : b * rows + half]
            bottom = query_total[:, b * rows + half : b * rows + rows]
            out_ref[place + b, half:rows, :] = (
                jnp.concatenate([top, bottom], axis=0).T.astype(bf16)
            )
    scale = jnp.where(low_lanes((1, LANES)), history_scale * 0.0625, history_scale)
    for block in range(blocks):
        out_ref[(block - shift) % blocks, 0:half, :] = (
            total_s[block * half : block * half + half, :] * scale
        ).astype(bf16)


def input_grad_kernel(shift, got_ref, proj_ref, target_ref, quarter_ref, digits_ref, send_ref):
    count, rows = got_ref.shape[0:2]
    half = rows // 2
    queries, keys, values = [], [], []
    for pair in range(HEADS // 2):
        query, joint = [], []
        for odd in range(2):
            slot = (2 * (2 * pair + odd) - shift) % count
            query.append(
                got_ref[slot, half:rows, :].astype(f32) + got_ref[slot + 1, half:rows, :].astype(f32)
            )
            joint.append(
                jnp.concatenate(
                    [got_ref[slot, 0:half, :], got_ref[slot + 1, 0:half, :]], axis=0
                ).astype(f32)
            )
        queries.append(jnp.concatenate([pair_low(*query), pair_high(*query)], axis=0))
        keys.append(pair_low(*joint))
        values.append(pair_high(*joint))
    stacked = jnp.concatenate(queries + keys + values, axis=1).astype(bf16)
    input_grad = lax.dot_general(
        stacked, proj_ref[...], (((1,), (1,)), ((), ())), preferred_element_type=f32
    ).astype(bf16)
    owners, pieces, lines = send_ref.shape[0:3]
    groups = (pieces - 1) * LANES // input_grad.shape[1]
    slots = groups * owners * lines

    def placed(at_ref, places, values):
        onehot = lax.broadcasted_iota(jnp.int32, (places, rows), 0) == at_ref[...]
        return jnp.dot(onehot.astype(f32).astype(bf16), values, preferred_element_type=f32)

    send_rows = placed(target_ref, slots, input_grad).reshape(owners, groups, lines, -1)
    for piece in range(pieces - 1):
        at = piece // groups * LANES
        send_ref[:, piece] = send_rows[:, piece % groups, :, at : at + LANES].astype(bf16)
    digits = placed(quarter_ref, slots // groups, digits_ref[...]).reshape(owners, lines, LANES)
    send_ref[:, pieces - 1] = digits.astype(bf16)


def slot_rows(digits, slab_rows):
    digits = digits.astype(f32)
    row = digits[:, 0:1] * DIGIT + digits[:, 1:2] - DIGIT
    lane = lax.broadcasted_iota(jnp.int32, (digits.shape[0], slab_rows), 1).astype(f32)
    return (row == lane).astype(f32).astype(bf16)


def slab_kernel(got_ref, slab_ref, digits_ref):
    owners, pieces, lines = got_ref.shape[0:3]
    slab_rows, features = slab_ref.shape
    groups = (pieces - 1) * LANES // features
    first = got_ref[:, pieces - 1].astype(f32).reshape(owners * lines, LANES)
    spread = [first]
    for group in range(1, groups):
        spread.append(pltpu.roll(first, LANES - 2 * group, 1))
    spread = [digits.reshape(owners, lines, LANES) for digits in spread]
    digits = jnp.concatenate(spread, axis=1).reshape(groups * owners * lines, LANES).astype(bf16)
    digits_ref[...] = digits
    select = slot_rows(digits, slab_rows)
    for column in range(features // LANES):
        parts = [got_ref[:, groups * column + group].astype(f32) for group in range(groups)]
        got = jnp.concatenate(parts, axis=1).reshape(digits.shape).astype(bf16)
        slab_ref[:, column * LANES : column * LANES + LANES] = lax.dot_general(
            select, got, (((0,), (0,)), ((), ())), preferred_element_type=f32
        ).astype(bf16)


def sum_kernel(got_ref, out_ref):
    count = got_ref.shape[0]
    total = got_ref[0].astype(f32)
    for source in range(1, count):
        total += got_ref[source].astype(f32)
    total = total.astype(bf16)
    for target in range(count):
        out_ref[target] = total


def adam_kernel(
    grad_ref, moment_ref, second_ref, table_ref, digits_ref,
    new_table_ref, new_moment_ref, new_second_ref, reply_ref,
):
    item_grad = grad_ref[...].astype(f32)
    mean = jnp.mean(item_grad * item_grad, axis=1, keepdims=True)
    new_second = second_decay * second_ref[:, 0:1] + (1.0 - second_decay) * mean
    new_second_ref[...] = jnp.broadcast_to(new_second, second_ref.shape).T[0:1]
    rate = step_rate / (jnp.sqrt(new_second) + epsilon)
    new_moment = first_decay * moment_ref[...] + (1.0 - first_decay) * item_grad
    new_moment_ref[...] = new_moment
    new_table = (table_ref[...].astype(f32) - new_moment * rate).astype(bf16)
    new_table_ref[...] = new_table
    select = slot_rows(digits_ref[...], new_table.shape[0])
    reply_ref[...] = jnp.dot(select, new_table, preferred_element_type=f32).astype(bf16)


def event_kernel(target_ref, got_ref, out_ref):
    slots = got_ref.shape[0]
    rows = out_ref.shape[0]
    onehot = (
        lax.broadcasted_iota(jnp.int32, (slots, rows), 0) == target_ref[...]
    ).astype(f32).astype(bf16)
    out_ref[...] = lax.dot_general(
        onehot, got_ref[...], (((0,), (0,)), ((), ())), preferred_element_type=f32
    ).astype(bf16)


def limit(mib):
    return pltpu.CompilerParams(vmem_limit_bytes=mib * 1024 * 1024)


def whole(dims):
    return pl.BlockSpec(dims, lambda i: (0, 0))


def shape(dims, kind):
    return jax.ShapeDtypeStruct(dims, kind)


def exchange(array, axis, shift):
    count = array.shape[0]
    order = [[(member + shift) % count for member in range(count)]]
    return lax.all_to_all(
        array, axis, split_axis=0, concat_axis=0, axis_index_groups=order, tiled=True
    )


def body(events_x, proj, out_grad, block_mask, item_ids, owner_of, local_of, table, moment, second):
    tokens = events_x.shape[1]
    features = events_x.shape[2]
    seq_count = lax.axis_size("seq")
    owner_count = lax.axis_size("table")
    position = lax.axis_index("seq")
    slab_rows = table.shape[0]
    capacity = 2 * tokens // owner_count
    slots = owner_count * capacity
    half = tokens // 2
    seq_shift = seq_count // 2 + math.isqrt(seq_count) // 2
    table_shift = owner_count // 2 + 3

    send = pl.pallas_call(
        functools.partial(project_kernel, seq_shift),
        out_shape=shape((seq_count, tokens + half, LANES), bf16),
        compiler_params=limit(60), name="project",
    )(events_x[0], proj, out_grad[0])
    got = exchange(send, "seq", seq_shift)

    place_of = owner_of * slab_rows + local_of
    place = place_of[item_ids[0]]
    owners = place // slab_rows
    slab_index = place % slab_rows
    event = jnp.arange(tokens)
    earlier = (owners[:, None] == owners[None, :]) & (event[:, None] < event[None, :])
    rank = jnp.sum(earlier.astype(jnp.int32), axis=0)
    member = (owners - table_shift) % owner_count
    target = (member * capacity + rank)[None, :]
    groups = 4
    lines = capacity // groups
    quarter = (member * lines + rank % lines)[None, :]
    pieces = groups * (features // LANES) + 1
    first_lane = 2 * (rank // lines)
    lane = jnp.arange(LANES)[None, :]
    digits = jnp.where(
        lane == first_lane[:, None],
        (slab_index // DIGIT + 1)[:, None],
        jnp.where(lane == first_lane[:, None] + 1, (slab_index % DIGIT)[:, None], 0),
    ).astype(bf16)
    second_col = jnp.broadcast_to(second[:, None], (slab_rows, LANES))
    got, target, quarter, digits, second_col = lax.optimization_barrier(
        (got, target, quarter, digits, second_col)
    )
    block_ids = jnp.arange(seq_count)
    visible = (block_mask == 1) | (block_ids[:, None] == block_ids[None, :])
    seen = jnp.repeat(visible.T.astype(f32), tokens, axis=1)
    part = (position % 2).astype(jnp.int32).reshape(1)
    back = pl.pallas_call(
        functools.partial(attention_kernel, seq_shift),
        out_shape=shape((seq_count, tokens, LANES), bf16),
        in_specs=[
            pl.BlockSpec(memory_space=pltpu.SMEM),
            pl.BlockSpec(memory_space=pltpu.VMEM),
            pl.BlockSpec(memory_space=pltpu.VMEM),
        ],
        scratch_shapes=[
            pltpu.VMEM((seq_count * half, LANES), bf16),
            pltpu.VMEM((seq_count * half, LANES), bf16),
            pltpu.VMEM((seq_count * half, LANES), f32),
            pltpu.VMEM((half, seq_count * half), bf16),
        ],
        compiler_params=limit(24), name="attention",
    )(part, seen, got)
    got_back = exchange(back, "seq", seq_shift)

    send_rows = pl.pallas_call(
        functools.partial(input_grad_kernel, seq_shift),
        out_shape=shape((owner_count, pieces, lines, LANES), bf16),
        compiler_params=limit(12), name="input_grad",
    )(got_back, proj, target, quarter, digits)
    got_rows = exchange(send_rows, "table", table_shift)

    slab, got_digits = pl.pallas_call(
        slab_kernel,
        out_shape=(shape((slab_rows, features), bf16), shape((slots, LANES), bf16)),
        compiler_params=limit(8), name="slab",
    )(got_rows)
    share = slab_rows // seq_count
    parts = exchange(slab.reshape(seq_count, share, features), "seq", seq_shift)
    copies = pl.pallas_call(
        sum_kernel,
        out_shape=shape((seq_count, share, features), bf16),
        compiler_params=limit(8), name="row_sum",
    )(parts)
    item_grad = exchange(copies, "seq", seq_shift).reshape(slab_rows, features)

    new_table, new_moment, new_second, reply = pl.pallas_call(
        adam_kernel,
        out_shape=(
            shape((slab_rows, features), bf16),
            shape((slab_rows, features), f32),
            shape((1, slab_rows), f32),
            shape((slots, features), bf16),
        ),
        grid=(1,),
        in_specs=[
            whole((slab_rows, features)),
            whole((slab_rows, features)),
            whole((slab_rows, LANES)),
            whole((slab_rows, features)),
            whole((slots, LANES)),
        ],
        out_specs=(
            whole((slab_rows, features)),
            whole((slab_rows, features)),
            whole((1, slab_rows)),
            whole((slots, features)),
        ),
        compiler_params=limit(12), name="adam",
    )(item_grad, moment, second_col, table, got_digits)
    returned = exchange(reply.reshape(owner_count, capacity, features), "table", table_shift)
    event_rows = pl.pallas_call(
        event_kernel,
        out_shape=shape((tokens, features), bf16),
        compiler_params=limit(8), name="event_rows",
    )(target, returned.reshape(slots, features))
    return (new_table, new_moment, new_second[0], event_rows[None])


def solution(mesh):
    return jax.shard_map(
        body,
        mesh=mesh,
        in_specs=(
            P("table", "seq", None),
            P(),
            P("table", "seq", None),
            P(),
            P("table", "seq"),
            P(),
            P(),
            P("table", None),
            P("table", None),
            P("table"),
        ),
        out_specs=(P("table", None), P("table", None), P("table"), P("table", "seq", None)),
        check_vma=False,
    )
```

```python
import functools
import math

import jax
import jax.numpy as jnp
from jax import lax
from jax.experimental import pallas as pl
from jax.experimental.pallas import tpu as pltpu
from jax.sharding import PartitionSpec as P

HEADS = 8
LANES = 128
DIGIT = 16

first_decay = 0.9
second_decay = 0.99
step_rate = 0.05
epsilon = 1e-08

f32 = jnp.float32
bf16 = jnp.bfloat16


def swap_halves(block):
    half = block.shape[1] // 2
    return pltpu.roll(block, half, 1)


def low_lanes(shape):
    return lax.broadcasted_iota(jnp.int32, shape, 1) < shape[1] // 2


def pair_low(first, second):
    return jnp.where(low_lanes(first.shape), first, swap_halves(second))


def pair_high(first, second):
    return jnp.where(low_lanes(first.shape), swap_halves(first), second)


def project_kernel(shift, x_ref, proj_ref, grad_ref, send_ref):
    features = x_ref.shape[1]
    rows = x_ref.shape[0]
    half = rows // 2
    count = send_ref.shape[0]
    thirds = [
        jnp.dot(
            x_ref[...], proj_ref[:, third * features : third * features + features],
            preferred_element_type=f32,
        )
        for third in range(3)
    ]
    for pair in range(HEADS // 2):
        at = pair * LANES
        queries, keys, values = [third[:, at : at + LANES] for third in thirds]
        cot = grad_ref[:, at : at + LANES].astype(f32)
        for odd, join in ((0, pair_low), (1, pair_high)):
            query_grad = join(queries, cot).astype(bf16)
            key_value = join(keys, values).astype(bf16)
            for part in range(2):
                slot = (2 * (2 * pair + odd) + part - shift) % count
                send_ref[slot, 0:rows, :] = query_grad
                send_ref[slot, rows : rows + half, :] = key_value[part * half : part * half + half]


def attention_kernel(shift, part_ref, seen_ref, got_ref, out_ref, key_s, value_s, total_s, key_t):
    blocks = got_ref.shape[0]
    rows = out_ref.shape[1]
    half = rows // 2
    tile = 2 * rows
    history_scale = 1.0 / math.sqrt(rows * blocks)
    part = part_ref[0]
    low = low_lanes((half, LANES))
    for block in range(blocks):
        both = got_ref[(block - shift) % blocks, rows : rows + half, :]
        zero = jnp.zeros_like(both)
        key_s[block * half : block * half + half, :] = jnp.where(
            low, both * jnp.bfloat16(0.0625), zero
        )
        value_s[block * half : block * half + half, :] = jnp.where(low, zero, both)
    key_t[...] = key_s[...].astype(f32).T[0:half].astype(bf16)
    key_row = lax.broadcasted_iota(jnp.int32, (rows, tile), 0)
    query_col = lax.broadcasted_iota(jnp.int32, (rows, tile), 1)
    key_pos = (key_row // half) * rows + part * half + key_row % half
    causal = (key_pos <= query_col).astype(f32)
    for step in range(blocks // 2):
        first = step * rows
        count = first + rows
        place = (2 * step - shift) % blocks
        query_grad = got_ref[place : place + 2, 0:rows, :].reshape(tile, LANES)
        keys = key_s[0:count, :]
        half_scores = lax.dot_general(
            keys, query_grad, (((1,), (1,)), ((), ())), preferred_element_type=f32
        )
        weight_grad = lax.dot_general(
            value_s[0:count, :], query_grad, (((1,), (1,)), ((), ())), preferred_element_type=f32
        )
        seen = [
            jnp.broadcast_to(
                seen_ref[block : block + 1, step * tile : step * tile + tile], (half, tile)
            )
            for block in range(2 * step + 2)
        ]
        for b in range(2):
            seen[2 * step + b] = seen[2 * step + b] * causal[b * half : b * half + half]
        gate2 = (1.0 + jnp.tanh(half_scores)) * jnp.concatenate(seen, axis=0)
        weights = half_scores * gate2
        score_grad = (weight_grad * (gate2 + weights * (2.0 - gate2))).astype(bf16)
        weights = weights.astype(bf16)
        key_part = jnp.dot(score_grad, query_grad, preferred_element_type=f32)
        value_part = jnp.dot(weights, query_grad, preferred_element_type=f32)
        joined = jnp.where(low_lanes(key_part.shape), key_part, value_part)
        if step > 0:
            total_s[0:first, :] += joined[0:first]
        total_s[first:count, :] = joined[first:count]
        query_total = history_scale * jnp.dot(
            key_t[:, 0:count], score_grad, preferred_element_type=f32
        )
        for b in range(2):
            top = query_total[:, b * rows : b * rows + half]
            bottom = query_total[:, b * rows + half : b * rows + rows]
            out_ref[place + b, half:rows, :] = (
                jnp.concatenate([top, bottom], axis=0).T.astype(bf16)
            )
    scale = jnp.where(low_lanes((1, LANES)), history_scale * 0.0625, history_scale)
    for block in range(blocks):
        out_ref[(block - shift) % blocks, 0:half, :] = (
            total_s[block * half : block * half + half, :] * scale
        ).astype(bf16)


def input_grad_kernel(shift, got_ref, proj_ref, target_ref, quarter_ref, digits_ref, send_ref):
    count, rows = got_ref.shape[0:2]
    half = rows // 2
    queries, keys, values = [], [], []
    for pair in range(HEADS // 2):
        query, joint = [], []
        for odd in range(2):
            slot = (2 * (2 * pair + odd) - shift) % count
            query.append(
                got_ref[slot, half:rows, :].astype(f32) + got_ref[slot + 1, half:rows, :].astype(f32)
            )
            joint.append(
                jnp.concatenate(
                    [got_ref[slot, 0:half, :], got_ref[slot + 1, 0:half, :]], axis=0
                ).astype(f32)
            )
        queries.append(jnp.concatenate([pair_low(*query), pair_high(*query)], axis=0))
        keys.append(pair_low(*joint))
        values.append(pair_high(*joint))
    stacked = jnp.concatenate(queries + keys + values, axis=1).astype(bf16)
    input_grad = lax.dot_general(
        stacked, proj_ref[...], (((1,), (1,)), ((), ())), preferred_element_type=f32
    ).astype(bf16)
    owners, pieces, lines = send_ref.shape[0:3]
    groups = (pieces - 1) * LANES // input_grad.shape[1]
    slots = groups * owners * lines

    def placed(at_ref, places, values):
        onehot = lax.broadcasted_iota(jnp.int32, (places, rows), 0) == at_ref[...]
        return jnp.dot(onehot.astype(f32).astype(bf16), values, preferred_element_type=f32)

    send_rows = placed(target_ref, slots, input_grad).reshape(owners, groups, lines, -1)
    for piece in range(pieces - 1):
        at = piece // groups * LANES
        send_ref[:, piece] = send_rows[:, piece % groups, :, at : at + LANES].astype(bf16)
    digits = placed(quarter_ref, slots // groups, digits_ref[...]).reshape(owners, lines, LANES)
    send_ref[:, pieces - 1] = digits.astype(bf16)


def slot_rows(digits, slab_rows):
    digits = digits.astype(f32)
    row = digits[:, 0:1] * DIGIT + digits[:, 1:2] - DIGIT
    lane = lax.broadcasted_iota(jnp.int32, (digits.shape[0], slab_rows), 1).astype(f32)
    return (row == lane).astype(f32).astype(bf16)


def slab_kernel(got_ref, slab_ref, digits_ref):
    owners, pieces, lines = got_ref.shape[0:3]
    slab_rows, features = slab_ref.shape
    groups = (pieces - 1) * LANES // features
    first = got_ref[:, pieces - 1].astype(f32).reshape(owners * lines, LANES)
    spread = [first]
    for group in range(1, groups):
        spread.append(pltpu.roll(first, LANES - 2 * group, 1))
    spread = [digits.reshape(owners, lines, LANES) for digits in spread]
    digits = jnp.concatenate(spread, axis=1).reshape(groups * owners * lines, LANES).astype(bf16)
    digits_ref[...] = digits
    select = slot_rows(digits, slab_rows)
    for column in range(features // LANES):
        parts = [got_ref[:, groups * column + group].astype(f32) for group in range(groups)]
        got = jnp.concatenate(parts, axis=1).reshape(digits.shape).astype(bf16)
        slab_ref[:, column * LANES : column * LANES + LANES] = lax.dot_general(
            select, got, (((0,), (0,)), ((), ())), preferred_element_type=f32
        ).astype(bf16)


def sum_kernel(got_ref, out_ref):
    count = got_ref.shape[0]
    total = got_ref[0].astype(f32)
    for source in range(1, count):
        total += got_ref[source].astype(f32)
    total = total.astype(bf16)
    for target in range(count):
        out_ref[target] = total


def adam_kernel(
    grad_ref, moment_ref, second_ref, table_ref, digits_ref,
    new_table_ref, new_moment_ref, new_second_ref, reply_ref,
):
    item_grad = grad_ref[...].astype(f32)
    mean = jnp.mean(item_grad * item_grad, axis=1, keepdims=True)
    new_second = second_decay * second_ref[:, 0:1] + (1.0 - second_decay) * mean
    new_second_ref[...] = jnp.broadcast_to(new_second, second_ref.shape).T[0:1]
    rate = step_rate / (jnp.sqrt(new_second) + epsilon)
    new_moment = first_decay * moment_ref[...] + (1.0 - first_decay) * item_grad
    new_moment_ref[...] = new_moment
    new_table = (table_ref[...].astype(f32) - new_moment * rate).astype(bf16)
    new_table_ref[...] = new_table
    select = slot_rows(digits_ref[...], new_table.shape[0])
    reply_ref[...] = jnp.dot(select, new_table, preferred_element_type=f32).astype(bf16)


def event_kernel(target_ref, got_ref, out_ref):
    slots = got_ref.shape[0]
    rows = out_ref.shape[0]
    onehot = (
        lax.broadcasted_iota(jnp.int32, (slots, rows), 0) == target_ref[...]
    ).astype(f32).astype(bf16)
    out_ref[...] = lax.dot_general(
        onehot, got_ref[...], (((0,), (0,)), ((), ())), preferred_element_type=f32
    ).astype(bf16)


def limit(mib):
    return pltpu.CompilerParams(vmem_limit_bytes=mib * 1024 * 1024)


def whole(dims):
    return pl.BlockSpec(dims, lambda i: (0, 0))


def shape(dims, kind):
    return jax.ShapeDtypeStruct(dims, kind)


def exchange(array, axis, shift):
    count = array.shape[0]
    order = [[(member + shift) % count for member in range(count)]]
    return lax.all_to_all(
        array, axis, split_axis=0, concat_axis=0, axis_index_groups=order, tiled=True
    )


def body(events_x, proj, out_grad, block_mask, item_ids, owner_of, local_of, table, moment, second):
    tokens = events_x.shape[1]
    features = events_x.shape[2]
    seq_count = lax.axis_size("seq")
    owner_count = lax.axis_size("table")
    position = lax.axis_index("seq")
    slab_rows = table.shape[0]
    capacity = 2 * tokens // owner_count
    slots = owner_count * capacity
    half = tokens // 2
    seq_shift = seq_count // 2 + math.isqrt(seq_count) // 2
    table_shift = owner_count // 2 + 3

    send = pl.pallas_call(
        functools.partial(project_kernel, seq_shift),
        out_shape=shape((seq_count, tokens + half, LANES), bf16),
        compiler_params=limit(60), name="project",
    )(events_x[0], proj, out_grad[0])
    got = exchange(send, "seq", seq_shift)

    place_of = owner_of * slab_rows + local_of
    place = place_of[item_ids[0]]
    owners = place // slab_rows
    slab_index = place % slab_rows
    event = jnp.arange(tokens)
    earlier = (owners[:, None] == owners[None, :]) & (event[:, None] < event[None, :])
    rank = jnp.sum(earlier.astype(jnp.int32), axis=0)
    member = (owners - table_shift) % owner_count
    target = (member * capacity + rank)[None, :]
    groups = 4
    lines = capacity // groups
    quarter = (member * lines + rank % lines)[None, :]
    pieces = groups * (features // LANES) + 1
    first_lane = 2 * (rank // lines)
    lane = jnp.arange(LANES)[None, :]
    digits = jnp.where(
        lane == first_lane[:, None],
        (slab_index // DIGIT + 1)[:, None],
        jnp.where(lane == first_lane[:, None] + 1, (slab_index % DIGIT)[:, None], 0),
    ).astype(bf16)
    second_col = jnp.broadcast_to(second[:, None], (slab_rows, LANES))
    got, target, quarter, digits, second_col = lax.optimization_barrier(
        (got, target, quarter, digits, second_col)
    )
    block_ids = jnp.arange(seq_count)
    visible = (block_mask == 1) | (block_ids[:, None] == block_ids[None, :])
    seen = jnp.repeat(visible.T.astype(f32), tokens, axis=1)
    part = (position % 2).astype(jnp.int32).reshape(1)
    back = pl.pallas_call(
        functools.partial(attention_kernel, seq_shift),
        out_shape=shape((seq_count, tokens, LANES), bf16),
        in_specs=[
            pl.BlockSpec(memory_space=pltpu.SMEM),
            pl.BlockSpec(memory_space=pltpu.VMEM),
            pl.BlockSpec(memory_space=pltpu.VMEM),
        ],
        scratch_shapes=[
            pltpu.VMEM((seq_count * half, LANES), bf16),
            pltpu.VMEM((seq_count * half, LANES), bf16),
            pltpu.VMEM((seq_count * half, LANES), f32),
            pltpu.VMEM((half, seq_count * half), bf16),
        ],
        compiler_params=limit(24), name="attention",
    )(part, seen, got)
    got_back = exchange(back, "seq", seq_shift)

    send_rows = pl.pallas_call(
        functools.partial(input_grad_kernel, seq_shift),
        out_shape=shape((owner_count, pieces, lines, LANES), bf16),
        compiler_params=limit(12), name="input_grad",
    )(got_back, proj, target, quarter, digits)
    got_rows = exchange(send_rows, "table", table_shift)

    slab, got_digits = pl.pallas_call(
        slab_kernel,
        out_shape=(shape((slab_rows, features), bf16), shape((slots, LANES), bf16)),
        compiler_params=limit(8), name="slab",
    )(got_rows)
    share = slab_rows // seq_count
    parts = exchange(slab.reshape(seq_count, share, features), "seq", seq_shift)
    copies = pl.pallas_call(
        sum_kernel,
        out_shape=shape((seq_count, share, features), bf16),
        compiler_params=limit(8), name="row_sum",
    )(parts)
    item_grad = exchange(copies, "seq", seq_shift).reshape(slab_rows, features)

    new_table, new_moment, new_second, reply = pl.pallas_call(
        adam_kernel,
        out_shape=(
            shape((slab_rows, features), bf16),
            shape((slab_rows, features), f32),
            shape((1, slab_rows), f32),
            shape((slots, features), bf16),
        ),
        grid=(1,),
        in_specs=[
            whole((slab_rows, features)),
            whole((slab_rows, features)),
            whole((slab_rows, LANES)),
            whole((slab_rows, features)),
            whole((slots, LANES)),
        ],
        out_specs=(
            whole((slab_rows, features)),
            whole((slab_rows, features)),
            whole((1, slab_rows)),
            whole((slots, features)),
        ),
        compiler_params=limit(12), name="adam",
    )(item_grad, moment, second_col, table, got_digits)
    returned = exchange(reply.reshape(owner_count, capacity, features), "table", table_shift)
    event_rows = pl.pallas_call(
        event_kernel,
        out_shape=shape((tokens, features), bf16),
        compiler_params=limit(8), name="event_rows",
    )(target, returned.reshape(slots, features))
    return (new_table, new_moment, new_second[0], event_rows[None])


def solution(mesh):
    return jax.shard_map(
        body,
        mesh=mesh,
        in_specs=(
            P("table", "seq", None),
            P(),
            P("table", "seq", None),
            P(),
            P("table", "seq"),
            P(),
            P(),
            P("table", None),
            P("table", None),
            P("table"),
        ),
        out_specs=(P("table", None), P("table", None), P("table"), P("table", "seq", None)),
        check_vma=False,
    )
```
